128 devices in a mesh: row: 8 (over y, z_hi), col: 16 (over z_lo, x, core).
Axes of the slice: x: 4, y: 4, z: 4 (z_hi: 2, z_lo: 2; z = z_hi * 2 + z_lo), core: 2. Of those that a mesh axis runs over, the one named last changes fastest.
Arguments:
- primal: float32 [16, 1024, 1024], P('col'), as said below
- dual_inv: float32 [16, 1024, 1024], P('col'), as said below
- col_values: bfloat16 [16, 16, 128, 4096], P(None, None, 'col'), as said below
- col_perm: int32 [16, 2048], replicated, may hold values from 0 to 2047, each once within a row
- slab_values: bfloat16 [16, 512, 4096], P('col', 'row'), as said below
- slab_tile: int32 [16, 512], P('col', 'row'), may hold values from 0 to 15
Outputs:
- schur_cyclic: float32 [512, 2048], P('row', 'col')
The draws below stay inside these ranges and needn't reach their ends.
Inputs may be any that keep to these rules, and one draw needn't show every extreme that they name: Each block's row of col_perm names every constraint exactly once. Each block of primal is symmetric. Each block of dual_inv is symmetric. `col_values`: every tile, read row-major as 64 x 64, is symmetric. `slab_values`: every tile, read row-major as 64 x 64, is symmetric.
All inputs are finite; a program needn't handle non-finite values.
Results may differ from the reference program's by a relative error of at most 0.0021.
Values may be sent and summed in bfloat16 or wider, within the bound.
No kernel may reach another device: no remote copies, remote signals or barrier semaphores. Data moves between devices by JAX's collectives and lax.ppermute only.
A program may use at most 256 MiB of HBM per device.

```python
import jax
import jax.numpy as jnp
from jax import lax

NB = 1024
TILE = 64
TN = 16
S_DEV = 64
NBLK = 16
MT = 128
M = 2048
S = 512
RB = 8
N_ROW = 8


def draw_primal(key, part):
    key = jax.random.fold_in(key, 11)
    first, second = jax.random.split(key)
    noise = 0.05 * jax.random.normal(first, (NBLK, NB, NB), jnp.float32)
    noise = (noise + jnp.swapaxes(noise, 1, 2)) * 0.7071
    diagonal = jax.random.uniform(second, (NBLK, NB), jnp.float32, 3.0, 6.0)
    return noise + diagonal[:, :, None] * jnp.eye(NB, dtype=jnp.float32)


def draw_dual_inv(key, part):
    key = jax.random.fold_in(key, 23)
    first, second = jax.random.split(key)
    noise = 0.05 * jax.random.normal(first, (NBLK, NB, NB), jnp.float32)
    noise = (noise + jnp.swapaxes(noise, 1, 2)) * 0.7071
    diagonal = jax.random.uniform(second, (NBLK, NB), jnp.float32, 3.0, 6.0)
    return noise + diagonal[:, :, None] * jnp.eye(NB, dtype=jnp.float32)


def draw_col_values(key, part):
    key = jax.random.fold_in(key, 37)
    noise = 0.03 * jax.random.normal(key, (NBLK, TN, MT, TILE, TILE), jnp.float32)
    square = (noise + jnp.swapaxes(noise, 3, 4)) * 0.7071
    return square.reshape(NBLK, TN, MT, TILE * TILE).astype(jnp.bfloat16)


def draw_slab_values(key, part):
    key = jax.random.fold_in(key, 41)
    noise = 0.03 * jax.random.normal(key, (NBLK, S, TILE, TILE), jnp.float32)
    square = (noise + jnp.swapaxes(noise, 2, 3)) * 0.7071
    return square.reshape(NBLK, S, TILE * TILE).astype(jnp.bfloat16)


def touch_ends(array, key, smallest, largest):
    shape = array.shape
    place = [jax.random.randint(jax.random.fold_in(key, axis), (), 0, shape[axis]) for axis in range(len(shape))]
    array = array.at[tuple(place)].set(smallest)
    longest = shape.index(max(shape))
    place[longest] = (place[longest] + 1) % shape[longest]
    return array.at[tuple(place)].set(largest)


def setup_inputs(seed: int = 0) -> dict:
    key_of = jax.random.split(jax.random.key(seed), 7)
    primal = draw_primal(jax.random.fold_in(key_of[6], 71), 0)
    dual_inv = draw_dual_inv(jax.random.fold_in(key_of[6], 71), 0)
    col_values = draw_col_values(jax.random.fold_in(key_of[6], 71), 0)
    col_perm = jax.vmap(lambda own: jax.random.permutation(own, M))(jax.random.split(key_of[3], NBLK)).reshape((NBLK, M)).astype(jnp.int32)
    slab_values = draw_slab_values(jax.random.fold_in(key_of[6], 71), 0)
    slab_tile = touch_ends(jax.random.randint(key_of[5], (NBLK, S), 0, TN), jax.random.fold_in(key_of[5], 1), 0, TN - 1).astype(jnp.int32)
    return dict(primal=primal, dual_inv=dual_inv, col_values=col_values, col_perm=col_perm, slab_values=slab_values, slab_tile=slab_tile)


HIGHEST = lax.Precision.HIGHEST


def block_terms(primal_block, dual_block, slab_block, tiles_block):
    order = primal_block.shape[0]
    tile_size = order // (order // TILE)
    tile_count = order // tile_size
    slab_square = slab_block.reshape(-1, tile_size, tile_size)
    primal_rows = jnp.take(primal_block.reshape(tile_count, tile_size, order), tiles_block, axis=0)
    dual_rows = jnp.take(dual_block.reshape(tile_count, tile_size, order), tiles_block, axis=0)
    panel = jnp.einsum("sac,scn->san", slab_square.astype(jnp.float32), dual_rows, precision=HIGHEST)
    primal_split = primal_rows.reshape(-1, tile_size, tile_count, tile_size)
    panel_split = panel.reshape(-1, tile_size, tile_count, tile_size)
    terms = jnp.einsum("scue,scuf->suef", primal_split, panel_split, precision=HIGHEST)
    return terms.reshape(terms.shape[0], tile_count, tile_size * tile_size).astype(jnp.bfloat16)


def reference(primal, dual_inv, col_values, col_perm, slab_values, slab_tile):
    def step(total, index):
        terms = block_terms(primal[index], dual_inv[index], slab_values[index], slab_tile[index])
        contrib = jnp.einsum("sup,ukp->suk", terms.astype(jnp.float32), col_values[index].astype(jnp.float32), precision=HIGHEST)
        flat = contrib.reshape(contrib.shape[0], -1)
        placed = jnp.zeros_like(total).at[:, col_perm[index]].set(flat)
        return total + placed, None

    start_total = jnp.zeros((slab_values.shape[1], col_perm.shape[1]), jnp.float32)
    total, unused = lax.scan(step, start_total, jnp.arange(NBLK))
    blocked = total.reshape(S_DEV // RB, N_ROW, RB, total.shape[1])
    return jnp.transpose(blocked, (1, 0, 2, 3)).reshape(total.shape[0], total.shape[1])
```

```python
import functools

import jax
import jax.numpy as jnp
from jax import lax
from jax.experimental import pallas as pl
from jax.experimental.pallas import tpu as pltpu
from jax.sharding import PartitionSpec as P

TILE = 64
HALF = TILE // 2
LANES = 128
PACKED = TILE * HALF + LANES
SPLIT = 4
F32 = jnp.float32
BF16 = jnp.bfloat16


def lane_parts(shape, first_vreg):
    lane = lax.broadcasted_iota(jnp.int32, shape, len(shape) - 1)
    e = lane // TILE + 2 * first_vreg
    h = (lane % TILE) // HALF
    f = lane % HALF
    return e, h, f


def pack_kernel(y_ref, values_ref, out_ref):
    blocks, groups, rows, width = values_ref.shape
    vregs = width // 2 // LANES
    shape = (2 * rows, LANES)
    for b in range(blocks):
        for g in range(0, groups, 2):
            extra = jnp.zeros(shape, F32)

            def load(start):
                return jnp.concatenate(
                    [
                        values_ref[b, g + s, :, start : start + LANES].astype(F32)
                        for s in range(2)
                    ],
                    axis=0,
                )

            for j in range(vregs):
                e, h, f = lane_parts(shape, j)
                upper = load(j * LANES)
                lower = pltpu.roll(load(width // 2 + j * LANES), LANES - HALF, 1)
                kept = jnp.where((h == 1) | (e <= f), upper, lower)
                extra = jnp.where((h == 0) & (e == f), lower, extra)
                out_ref[b, g * rows : (g + 2) * rows, j * LANES : (j + 1) * LANES] = kept.astype(BF16)
            out_ref[b, g * rows : (g + 2) * rows, vregs * LANES :] = extra.astype(BF16)


def pack(y, values):
    blocks, tiles, rows, width = values.shape
    groups = tiles // SPLIT
    step = 2
    return pl.pallas_call(
        pack_kernel,
        out_shape=jax.ShapeDtypeStruct((blocks, groups * rows, PACKED), BF16),
        grid_spec=pltpu.PrefetchScalarGridSpec(
            num_scalar_prefetch=1,
            grid=(blocks // step,),
            in_specs=[pl.BlockSpec((step, groups, rows, width), lambda g, y: (g, y[0], 0, 0))],
            out_specs=pl.BlockSpec((step, groups * rows, PACKED), lambda g, y: (g, 0, 0)),
        ),
        cost_estimate=pl.CostEstimate(flops=10**7, transcendentals=0, bytes_accessed=7 * 10**6),
        name="pack",
    )(y, values)


def split2(x):
    high = x.astype(BF16)
    low = (x - high.astype(F32)).astype(BF16)
    return high, low


ROWS = 16
UNROLL = 4


def terms_kernel(y_ref, tile_ref, primal_ref, dual_ref, slab_ref, out_ref, dual_w, primal_w, stage, terms):
    tiles = dual_w.shape[0]
    groups = out_ref.shape[0]
    low_lanes = lax.broadcasted_iota(jnp.int32, (HALF, LANES), 1) < TILE

    @pl.when(pl.program_id(0) == 0)
    def prepare():
        for t in range(tiles):
            high, low = split2(dual_ref[0, t * TILE : (t + 1) * TILE, :])
            dual_w[t, :TILE, :] = high
            dual_w[t, TILE:, :] = low
        for j in range(tiles // 2):
            stage[j] = primal_ref[0, :, j * LANES : (j + 1) * LANES]
        for u in range(groups):
            for par in range(2):
                rows = pl.ds(u * TILE + par * HALF, HALF)
                for j in range(tiles // 2):
                    x = stage[j, pl.ds(u * TILE + par, HALF, stride=2), :]
                    for place, part in enumerate(split2(x)):
                        part = part.astype(F32)
                        turned = pltpu.roll(part, TILE, 1)
                        lanes = slice(place * LANES, (place + 1) * LANES)
                        primal_w[2 * j, rows, lanes] = jnp.where(low_lanes, part, turned).astype(BF16)
                        primal_w[2 * j + 1, rows, lanes] = jnp.where(low_lanes, turned, part).astype(BF16)

    first = pl.program_id(0) * ROWS

    def some_rows(step, carry):
        for inner in range(UNROLL):
            i = step * UNROLL + inner
            t = tile_ref[first + i]
            z = slab_ref[pl.ds(pl.multiple_of(i * HALF, HALF), HALF), :].astype(F32)
            turned = pltpu.roll(z, TILE, 1)
            square = jnp.concatenate(
                [
                    jnp.where(low_lanes, z, turned).astype(BF16),
                    jnp.where(low_lanes, turned, z).astype(BF16),
                ],
                axis=0,
            )
            panel = jnp.dot(square, dual_w[t], preferred_element_type=F32)
            high, low = split2(panel)
            weights = jnp.concatenate([high, low, high, low], axis=0)
            for pair in range(groups // 2):
                lanes = slice(pair * LANES, (pair + 1) * LANES)
                out = jnp.dot(
                    primal_w[t, pair * LANES : (pair + 1) * LANES, :],
                    weights[:, lanes],
                    preferred_element_type=F32,
                )
                even0, odd0, even1, odd1 = (out[q * HALF : (q + 1) * HALF] for q in range(4))
                mixed = pltpu.roll(jnp.where(low_lanes, odd0, even1), TILE, 1)
                terms[2 * pair, pl.ds(i, HALF, stride=ROWS), :] = jnp.where(low_lanes, even0, mixed)
                terms[2 * pair + 1, pl.ds(i, HALF, stride=ROWS), :] = jnp.where(low_lanes, mixed, odd1)
        return carry

    lax.fori_loop(0, ROWS // UNROLL, some_rows, 0)
    for u in range(groups):
        for m in range(HALF):
            out_ref[u, :, m * LANES : (m + 1) * LANES] = terms[u, m * ROWS : (m + 1) * ROWS, :].astype(BF16)


def make_terms(y, tile_of, primal, dual, slab):
    order = primal.shape[1]
    tiles = order // TILE
    groups = tiles // SPLIT
    count = tile_of.shape[0]
    width = groups * TILE
    return pl.pallas_call(
        terms_kernel,
        out_shape=jax.ShapeDtypeStruct((groups, count, TILE * TILE), BF16),
        grid_spec=pltpu.PrefetchScalarGridSpec(
            num_scalar_prefetch=2,
            grid=(count // ROWS,),
            in_specs=[
                pl.BlockSpec((1, width, order), lambda g, y, t: (0, y[0], 0)),
                pl.BlockSpec((1, order, width), lambda g, y, t: (0, 0, y[0])),
                pl.BlockSpec((ROWS * HALF, LANES), lambda g, y, t: (g, 0)),
            ],
            out_specs=pl.BlockSpec((groups, ROWS, TILE * TILE), lambda g, y, t: (0, g, 0)),
            scratch_shapes=[
                pltpu.VMEM((tiles, 2 * TILE, width), BF16),
                pltpu.VMEM((tiles, width, 4 * TILE), BF16),
                pltpu.VMEM((tiles // 2, width, LANES), F32),
                pltpu.VMEM((groups, HALF * ROWS, LANES), F32),
            ],
        ),
        compiler_params=pltpu.CompilerParams(vmem_limit_bytes=40 << 20),
        cost_estimate=pl.CostEstimate(
            flops=count * 10**8, transcendentals=0, bytes_accessed=2 * 10**6 + count * 40000
        ),
        name="terms",
    )(y, tile_of, primal, dual, slab)


def turn_matrix():
    source = lax.broadcasted_iota(jnp.int32, (PACKED, TILE * HALF), 0)
    target = lax.broadcasted_iota(jnp.int32, (PACKED, TILE * HALF), 1)
    e, h, f = target // TILE, (target % TILE) // HALF, target % HALF
    plain = f * TILE + h * HALF + e
    diagonal = TILE * HALF + (e % 2) * TILE + e
    wanted = jnp.where((h == 0) & (e == f), diagonal, plain)
    return (source == wanted).astype(BF16)


STEP = 256


def contract_kernel(packed_ref, part_ref, turn_ref, *refs):
    own_up, own_low, rest_up, rest_low, out_ref, acc = refs
    step = pl.program_id(0)
    groups = own_up.shape[0]
    count = packed_ref.shape[0]
    rows = packed_ref.shape[1]
    small = rows // groups

    @pl.when(step == 0)
    def clear():
        acc[...] = jnp.zeros_like(acc)

    flat = packed_ref[...].reshape(count * rows, PACKED)
    turned = jnp.dot(flat, turn_ref[...], preferred_element_type=F32)
    plain = part_ref[...].reshape(count * rows, STEP).astype(F32)
    low_rows, up_rows = [], []
    for half in range(STEP // LANES):
        lanes = slice(half * LANES, (half + 1) * LANES)
        g, t = plain[:, lanes], turned[:, lanes]
        lane = lax.broadcasted_iota(jnp.int32, g.shape, 1)
        e = lane // TILE + 2 * half + step * (STEP // TILE)
        h = (lane % TILE) // HALF
        f = lane % HALF
        up_rows.append(jnp.where((h == 0) & (e > f), t, g))
        mixed = jnp.where((h == 0) & (e > f), g, t)
        low_rows.append(
            jnp.where(h == 0, pltpu.roll(mixed, LANES - HALF, 1), pltpu.roll(mixed, HALF, 1))
        )
    upper = jnp.concatenate(up_rows, axis=1).reshape(count, groups, small, STEP)
    lower = jnp.concatenate(low_rows, axis=1).reshape(count, groups, small, STEP)
    nt = (((1,), (1,)), ((), ()))
    for u in range(groups):
        weights_up = upper[:, u].reshape(count * small, STEP).astype(BF16)
        weights_low = lower[:, u].reshape(count * small, STEP).astype(BF16)
        left_up = jnp.concatenate([own_up[u], rest_up[u]], axis=0)
        left_low = jnp.concatenate([own_low[u], rest_low[u]], axis=0)
        acc[u] += lax.dot_general(
            left_up, weights_up, nt, preferred_element_type=F32
        ) + lax.dot_general(left_low, weights_low, nt, preferred_element_type=F32)

    @pl.when(step == pl.num_programs(0) - 1)
    def finish():
        targets, sources, _ = out_ref.shape
        for u in range(groups):
            for s in range(sources // 8):
                for r in range(targets):
                    start = (s * targets + r) * 8
                    out_ref[r, s * 8 : (s + 1) * 8, u * LANES : (u + 1) * LANES] = acc[u, start : start + 8, :]


def contract(packed, turn, own, rest, targets):
    count, rows, _ = packed.shape
    groups, own_rows, width = own.shape
    rest_rows = rest.shape[1]
    total = own_rows + rest_rows
    steps = width // 2 // STEP
    return pl.pallas_call(
        contract_kernel,
        out_shape=jax.ShapeDtypeStruct((targets, total // targets, groups * LANES), F32),
        grid_spec=pltpu.PrefetchScalarGridSpec(
            num_scalar_prefetch=0,
            grid=(steps,),
            in_specs=[
                pl.BlockSpec((count, rows, PACKED), lambda g: (0, 0, 0)),
                pl.BlockSpec((count, rows, STEP), lambda g: (0, 0, g)),
                pl.BlockSpec((PACKED, STEP), lambda g: (0, g)),
                pl.BlockSpec((groups, own_rows, STEP), lambda g: (0, 0, g)),
                pl.BlockSpec((groups, own_rows, STEP), lambda g: (0, 0, g + steps)),
                pl.BlockSpec((groups, rest_rows, STEP), lambda g: (0, 0, g)),
                pl.BlockSpec((groups, rest_rows, STEP), lambda g: (0, 0, g + steps)),
            ],
            out_specs=pl.BlockSpec((targets, total // targets, groups * LANES), lambda g: (0, 0, 0)),
            scratch_shapes=[pltpu.VMEM((groups, total, LANES), F32)],
        ),
        compiler_params=pltpu.CompilerParams(vmem_limit_bytes=40 << 20),
        cost_estimate=pl.CostEstimate(flops=6 * 10**9, transcendentals=0, bytes_accessed=2 * 10**7),
        name="contract",
    )(packed, packed, turn, own, own, rest, rest)


def place_kernel(perm_ref, parts_ref, out_ref, left):
    step = pl.program_id(0)
    sources, rows, width = parts_ref.shape
    total = sources * 8

    @pl.when(step == 0)
    def prepare():
        for y_s in range(SPLIT):
            for z in range(sources // SPLIT):
                for y in range(SPLIT):
                    d = (y_s - y) % SPLIT
                    value = parts_ref[y_s * (sources // SPLIT) + z, d * 8 : (d + 1) * 8, :]
                    start = (y * (sources // SPLIT) + z) * 8
                    left[start : start + 8, y_s * width : (y_s + 1) * width] = value

    value = left[...]
    high = value.astype(BF16)
    value = value - high.astype(F32)
    middle = value.astype(BF16)
    low = (value - middle.astype(F32)).astype(BF16)
    pieces = jnp.concatenate([high, middle, low], axis=0)
    target = lax.broadcasted_iota(jnp.int32, (STEP, perm_ref.shape[1]), 0) + step * STEP
    chosen = jnp.where(perm_ref[...] == target, 1.0, 0.0).astype(BF16)
    out = lax.dot_general(pieces, chosen, (((1,), (1,)), ((), ())), preferred_element_type=F32)
    out = out[:total] + out[total : 2 * total] + out[2 * total :]
    for c in range(STEP // LANES):
        out_ref[c] = out[:, c * LANES : (c + 1) * LANES]


def place(perm, parts):
    sources, rows, width = parts.shape
    columns = perm.shape[1]
    total = sources * 8
    return pl.pallas_call(
        place_kernel,
        out_shape=jax.ShapeDtypeStruct((columns // LANES, total, LANES), F32),
        grid_spec=pltpu.PrefetchScalarGridSpec(
            num_scalar_prefetch=0,
            grid=(columns // STEP,),
            in_specs=[
                pl.BlockSpec((1, columns), lambda g: (0, 0)),
                pl.BlockSpec((sources, rows, width), lambda g: (0, 0, 0)),
            ],
            out_specs=pl.BlockSpec((STEP // LANES, total, LANES), lambda g: (g, 0, 0)),
            scratch_shapes=[pltpu.VMEM((total, columns), F32)],
        ),
        compiler_params=pltpu.CompilerParams(vmem_limit_bytes=40 << 20),
        cost_estimate=pl.CostEstimate(flops=2 * 10**9, transcendentals=0, bytes_accessed=10**6),
        name="place",
    )(perm, parts)


def body(row_size, primal, dual_inv, col_values, col_perm, slab_values, slab_tile):
    count = slab_values.shape[1]
    tiles = col_values.shape[1]
    shared = row_size // SPLIT
    block = lax.axis_index("col")
    y = (lax.axis_index("row") // shared).astype(jnp.int32).reshape(1)

    square = slab_values[0].reshape(count, 2, HALF, TILE)
    square = jnp.concatenate([square[:, 0], square[:, 1]], axis=2)
    own_tile = slab_tile[0]
    row = jnp.zeros((16, LANES), BF16).at[0, :count].set(own_tile.astype(BF16))
    own_slab = square.reshape(count * HALF, LANES)
    message = jnp.concatenate([own_slab, row], axis=0)
    arrived = []
    for d in range(1, SPLIT):
        pairs = [(i, (i + d * shared) % row_size) for i in range(row_size)]
        arrived.append(lax.ppermute(message, "row", pairs))

    packed = pack(y, col_values)
    packed = lax.all_to_all(packed, "col", split_axis=0, concat_axis=0, tiled=True)

    own = make_terms(y, own_tile, primal, dual_inv, own_slab)
    rest_slab = jnp.concatenate([m[: count * HALF] for m in arrived], axis=0)
    rest_tile = jnp.concatenate([m[count * HALF, :count] for m in arrived]).astype(jnp.int32)
    rest = make_terms(y, rest_tile, primal, dual_inv, rest_slab)
    parts = contract(packed, turn_matrix(), own, rest, row_size)
    parts = lax.all_to_all(parts, "row", split_axis=0, concat_axis=0, tiled=True)
    perm = lax.dynamic_slice_in_dim(col_perm, block, 1, axis=0)
    placed = place(perm, parts)
    placed = lax.all_to_all(placed, "col", split_axis=0, concat_axis=0, tiled=True)
    return jnp.sum(placed, axis=0)


def solution(mesh):
    return jax.shard_map(
        functools.partial(body, mesh.shape["row"]),
        mesh=mesh,
        in_specs=(
            P("col", None, None),
            P("col", None, None),
            P(None, None, "col", None),
            P(),
            P("col", "row", None),
            P("col", "row"),
        ),
        out_specs=P("row", "col"),
        check_vma=False,
    )
```

```python
import functools

import jax
import jax.numpy as jnp
from jax import lax
from jax.experimental import pallas as pl
from jax.experimental.pallas import tpu as pltpu
from jax.sharding import PartitionSpec as P

TILE = 64
HALF = TILE // 2
LANES = 128
PACKED = TILE * HALF + LANES
SPLIT = 4
F32 = jnp.float32
BF16 = jnp.bfloat16


def lane_parts(shape, first_vreg):
    lane = lax.broadcasted_iota(jnp.int32, shape, len(shape) - 1)
    e = lane // TILE + 2 * first_vreg
    h = (lane % TILE) // HALF
    f = lane % HALF
    return e, h, f


def pack_kernel(y_ref, values_ref, out_ref):
    blocks, groups, rows, width = values_ref.shape
    vregs = width // 2 // LANES
    shape = (2 * rows, LANES)
    for b in range(blocks):
        for g in range(0, groups, 2):
            extra = jnp.zeros(shape, F32)

            def load(start):
                return jnp.concatenate(
                    [
                        values_ref[b, g + s, :, start : start + LANES].astype(F32)
                        for s in range(2)
                    ],
                    axis=0,
                )

            for j in range(vregs):
                e, h, f = lane_parts(shape, j)
                upper = load(j * LANES)
                lower = pltpu.roll(load(width // 2 + j * LANES), LANES - HALF, 1)
                kept = jnp.where((h == 1) | (e <= f), upper, lower)
                extra = jnp.where((h == 0) & (e == f), lower, extra)
                out_ref[b, g * rows : (g + 2) * rows, j * LANES : (j + 1) * LANES] = kept.astype(BF16)
            out_ref[b, g * rows : (g + 2) * rows, vregs * LANES :] = extra.astype(BF16)


def pack(y, values):
    blocks, tiles, rows, width = values.shape
    groups = tiles // SPLIT
    step = 2
    return pl.pallas_call(
        pack_kernel,
        out_shape=jax.ShapeDtypeStruct((blocks, groups * rows, PACKED), BF16),
        grid_spec=pltpu.PrefetchScalarGridSpec(
            num_scalar_prefetch=1,
            grid=(blocks // step,),
            in_specs=[pl.BlockSpec((step, groups, rows, width), lambda g, y: (g, y[0], 0, 0))],
            out_specs=pl.BlockSpec((step, groups * rows, PACKED), lambda g, y: (g, 0, 0)),
        ),
        cost_estimate=pl.CostEstimate(flops=10**7, transcendentals=0, bytes_accessed=7 * 10**6),
        name="pack",
    )(y, values)


def split2(x):
    high = x.astype(BF16)
    low = (x - high.astype(F32)).astype(BF16)
    return high, low


ROWS = 16


def terms_kernel(parts, y_ref, *refs):
    tile_refs, primal_ref, dual_ref, slabs = refs[:parts], refs[parts], refs[parts + 1], refs[parts + 2 : -6]
    out_ref, dual_w, primal_w, stage, weights, terms = refs[-6:]
    tiles = dual_w.shape[0]
    groups = out_ref.shape[0]
    step = pl.program_id(0)
    steps = pl.num_programs(0) // len(slabs)
    low_lanes = lax.broadcasted_iota(jnp.int32, (HALF, LANES), 1) < TILE

    @pl.when(step == 0)
    def prepare():
        for t in range(tiles):
            high, low = split2(dual_ref[0, t * TILE : (t + 1) * TILE, :])
            dual_w[t, :TILE, :] = high
            dual_w[t, TILE:, :] = low
        source = lax.broadcasted_iota(jnp.int32, (LANES, 2 * LANES), 0)
        target = lax.broadcasted_iota(jnp.int32, (LANES, 2 * LANES), 1)
        wanted = (target // LANES) * TILE + 2 * (target % HALF) + (target % TILE) // HALF
        spread = jnp.where(source == wanted, 1.0, 0.0).astype(BF16)
        for j in range(tiles // 2):
            stage[...] = primal_ref[0, :, j * LANES : (j + 1) * LANES]
            x = jnp.concatenate(
                [
                    stage[pl.ds(u * TILE + par, HALF, stride=2), :]
                    for u in range(groups)
                    for par in range(2)
                ],
                axis=0,
            )
            for place, part in enumerate(split2(x)):
                part = jnp.dot(part, spread, preferred_element_type=F32).astype(BF16)
                lanes = slice(place * LANES, (place + 1) * LANES)
                primal_w[2 * j, :, lanes] = part[:, :LANES]
                primal_w[2 * j + 1, :, lanes] = part[:, LANES:]

    for k, slab_ref in enumerate(slabs):

        @pl.when(step // steps == k)
        def spread_rows():
            for m in range(HALF):
                terms[0, pl.ds(m, ROWS, stride=HALF), :] = slab_ref[0, :, m * LANES : (m + 1) * LANES].astype(F32)

    tile_of = []
    for i in range(ROWS):
        place = (step % steps) * ROWS + i
        t = tile_refs[0][0, place]
        for k in range(1, parts):
            t = jnp.where(step // steps == k, tile_refs[k][0, place], t)
        tile_of.append(t)

    for i in range(ROWS):
        z = terms[0, i * HALF : (i + 1) * HALF, :]
        turned = pltpu.roll(z, TILE, 1)
        square = jnp.concatenate(
            [
                jnp.where(low_lanes, z, turned).astype(BF16),
                jnp.where(low_lanes, turned, z).astype(BF16),
            ],
            axis=0,
        )
        panel = jnp.dot(square, dual_w[tile_of[i]], preferred_element_type=F32)
        high, low = split2(panel)
        weights[i, :TILE, :] = high
        weights[i, TILE:, :] = low

    for i in range(ROWS):
        t = tile_of[i]
        for pair in range(groups // 2):
            lanes = slice(pair * LANES, (pair + 1) * LANES)
            right = weights[i, :, lanes]
            out = jnp.dot(
                primal_w[t, pair * LANES : (pair + 1) * LANES, :],
                jnp.concatenate([right, right], axis=0),
                preferred_element_type=F32,
            )
            even0, odd0, even1, odd1 = (out[q * HALF : (q + 1) * HALF] for q in range(4))
            mixed = pltpu.roll(jnp.where(low_lanes, odd0, even1), TILE, 1)
            terms[2 * pair, pl.ds(i, HALF, stride=ROWS), :] = jnp.where(low_lanes, even0, mixed)
            terms[2 * pair + 1, pl.ds(i, HALF, stride=ROWS), :] = jnp.where(low_lanes, mixed, odd1)

    for u in range(groups):
        for m in range(HALF):
            out_ref[u, :, m * LANES : (m + 1) * LANES] = terms[u, m * ROWS : (m + 1) * ROWS, :].astype(BF16)


def make_terms(y, primal, dual, tile_of, slabs):
    order = primal.shape[1]
    tiles = order // TILE
    groups = tiles // SPLIT
    count = slabs[0].shape[1]
    steps = count // ROWS
    width = groups * TILE
    total = count * len(slabs)

    def slab_spec(k):
        return pl.BlockSpec(
            (1, ROWS, TILE * TILE),
            lambda g, *s: (0, jnp.clip(g - k * steps, 0, steps - 1), 0),
        )

    return pl.pallas_call(
        functools.partial(terms_kernel, len(slabs)),
        out_shape=jax.ShapeDtypeStruct((groups, total, TILE * TILE), BF16),
        grid_spec=pltpu.PrefetchScalarGridSpec(
            num_scalar_prefetch=1 + len(slabs),
            grid=(total // ROWS,),
            in_specs=[
                pl.BlockSpec((1, width, order), lambda g, y, *s: (0, y[0], 0)),
                pl.BlockSpec((1, order, width), lambda g, y, *s: (0, 0, y[0])),
                *(slab_spec(k) for k in range(len(slabs))),
            ],
            out_specs=pl.BlockSpec((groups, ROWS, TILE * TILE), lambda g, *s: (0, g, 0)),
            scratch_shapes=[
                pltpu.VMEM((tiles, 2 * TILE, width), BF16),
                pltpu.VMEM((tiles, width, 4 * TILE), BF16),
                pltpu.VMEM((width, LANES), F32),
                pltpu.VMEM((ROWS, 2 * TILE, width), BF16),
                pltpu.VMEM((groups, HALF * ROWS, LANES), F32),
            ],
        ),
        compiler_params=pltpu.CompilerParams(vmem_limit_bytes=61 << 20),
        cost_estimate=pl.CostEstimate(
            flops=total * 10**8, transcendentals=0, bytes_accessed=2 * 10**6 + total * 40000
        ),
        name="terms",
    )(y, *tile_of, primal, dual, *slabs)


STEP = 256


def contract_kernel(packed_ref, part_ref, *refs):
    own_up, own_low, rest_up, rest_low, out_ref, acc = refs
    step = pl.program_id(0)
    groups = own_up.shape[0]
    count = packed_ref.shape[0]
    rows = packed_ref.shape[1]
    small = rows // groups

    @pl.when(step == 0)
    def clear():
        acc[...] = jnp.zeros_like(acc)

    flat = packed_ref[...].reshape(count * rows, PACKED)
    target = lax.broadcasted_iota(jnp.int32, (1, STEP), 1)
    e = target // TILE + step * (STEP // TILE)
    h = (target % TILE) // HALF
    f = target % HALF
    wanted = jnp.where(
        (h == 0) & (e == f), TILE * HALF + (e % 2) * TILE + e, f * TILE + h * HALF + e
    )
    source = lax.broadcasted_iota(jnp.int32, (PACKED, STEP), 0)
    turn = jnp.where(source == wanted, 1.0, 0.0).astype(BF16)
    turned = jnp.dot(flat, turn, preferred_element_type=F32)
    plain = part_ref[...].reshape(count * rows, STEP).astype(F32)
    low_rows, up_rows = [], []
    for half in range(STEP // LANES):
        lanes = slice(half * LANES, (half + 1) * LANES)
        g, t = plain[:, lanes], turned[:, lanes]
        lane = lax.broadcasted_iota(jnp.int32, g.shape, 1)
        e = lane // TILE + 2 * half + step * (STEP // TILE)
        h = (lane % TILE) // HALF
        f = lane % HALF
        up_rows.append(jnp.where((h == 0) & (e > f), t, g))
        mixed = jnp.where((h == 0) & (e > f), g, t)
        low_rows.append(
            jnp.where(h == 0, pltpu.roll(mixed, LANES - HALF, 1), pltpu.roll(mixed, HALF, 1))
        )
    upper = jnp.concatenate(up_rows, axis=1).reshape(count, groups, small, STEP)
    lower = jnp.concatenate(low_rows, axis=1).reshape(count, groups, small, STEP)
    nt = (((1,), (1,)), ((), ()))
    for u in range(groups):
        weights_up = upper[:, u].reshape(count * small, STEP).astype(BF16)
        weights_low = lower[:, u].reshape(count * small, STEP).astype(BF16)
        left_up = jnp.concatenate([own_up[u], rest_up[u]], axis=0)
        left_low = jnp.concatenate([own_low[u], rest_low[u]], axis=0)
        acc[u] += lax.dot_general(
            left_up, weights_up, nt, preferred_element_type=F32
        ) + lax.dot_general(left_low, weights_low, nt, preferred_element_type=F32)

    @pl.when(step == pl.num_programs(0) - 1)
    def finish():
        targets, sources, _ = out_ref.shape
        for u in range(groups):
            for s in range(sources // 8):
                for r in range(targets):
                    start = (s * targets + r) * 8
                    out_ref[r, s * 8 : (s + 1) * 8, u * LANES : (u + 1) * LANES] = acc[u, start : start + 8, :]


def contract(packed, own, rest, targets):
    count, rows, _ = packed.shape
    groups, own_rows, width = own.shape
    rest_rows = rest.shape[1]
    total = own_rows + rest_rows
    steps = width // 2 // STEP
    return pl.pallas_call(
        contract_kernel,
        out_shape=jax.ShapeDtypeStruct((targets, total // targets, groups * LANES), F32),
        grid_spec=pltpu.PrefetchScalarGridSpec(
            num_scalar_prefetch=0,
            grid=(steps,),
            in_specs=[
                pl.BlockSpec((count, rows, PACKED), lambda g: (0, 0, 0)),
                pl.BlockSpec((count, rows, STEP), lambda g: (0, 0, g)),
                pl.BlockSpec((groups, own_rows, STEP), lambda g: (0, 0, g)),
                pl.BlockSpec((groups, own_rows, STEP), lambda g: (0, 0, g + steps)),
                pl.BlockSpec((groups, rest_rows, STEP), lambda g: (0, 0, g)),
                pl.BlockSpec((groups, rest_rows, STEP), lambda g: (0, 0, g + steps)),
            ],
            out_specs=pl.BlockSpec((targets, total // targets, groups * LANES), lambda g: (0, 0, 0)),
            scratch_shapes=[pltpu.VMEM((groups, total, LANES), F32)],
        ),
        compiler_params=pltpu.CompilerParams(vmem_limit_bytes=59 << 20),
        cost_estimate=pl.CostEstimate(flops=6 * 10**9, transcendentals=0, bytes_accessed=2 * 10**7),
        name="contract",
    )(packed, packed, own, own, rest, rest)


def place_kernel(perm_ref, parts_ref, out_ref, left):
    step = pl.program_id(0)
    sources, rows, width = parts_ref.shape
    total = sources * 8

    @pl.when(step == 0)
    def prepare():
        for y_s in range(SPLIT):
            for z in range(sources // SPLIT):
                for y in range(SPLIT):
                    d = (y_s - y) % SPLIT
                    value = parts_ref[y_s * (sources // SPLIT) + z, d * 8 : (d + 1) * 8, :]
                    start = (y * (sources // SPLIT) + z) * 8
                    left[start : start + 8, y_s * width : (y_s + 1) * width] = value

    value = left[...]
    high = value.astype(BF16)
    value = value - high.astype(F32)
    middle = value.astype(BF16)
    low = (value - middle.astype(F32)).astype(BF16)
    pieces = jnp.concatenate([high, middle, low], axis=0)
    target = lax.broadcasted_iota(jnp.int32, (STEP, perm_ref.shape[1]), 0) + step * STEP
    chosen = jnp.where(perm_ref[...] == target, 1.0, 0.0).astype(BF16)
    out = lax.dot_general(pieces, chosen, (((1,), (1,)), ((), ())), preferred_element_type=F32)
    out = out[:total] + out[total : 2 * total] + out[2 * total :]
    for c in range(STEP // LANES):
        out_ref[c] = out[:, c * LANES : (c + 1) * LANES]


def place(perm, parts):
    sources, rows, width = parts.shape
    columns = perm.shape[1]
    total = sources * 8
    return pl.pallas_call(
        place_kernel,
        out_shape=jax.ShapeDtypeStruct((columns // LANES, total, LANES), F32),
        grid_spec=pltpu.PrefetchScalarGridSpec(
            num_scalar_prefetch=0,
            grid=(columns // STEP,),
            in_specs=[
                pl.BlockSpec((1, columns), lambda g: (0, 0)),
                pl.BlockSpec((sources, rows, width), lambda g: (0, 0, 0)),
            ],
            out_specs=pl.BlockSpec((STEP // LANES, total, LANES), lambda g: (g, 0, 0)),
            scratch_shapes=[pltpu.VMEM((total, columns), F32)],
        ),
        compiler_params=pltpu.CompilerParams(vmem_limit_bytes=40 << 20),
        cost_estimate=pl.CostEstimate(flops=2 * 10**9, transcendentals=0, bytes_accessed=10**6),
        name="place",
    )(perm, parts)


def body(row_size, primal, dual_inv, col_values, col_perm, slab_values, slab_tile):
    count = slab_values.shape[1]
    shared = row_size // SPLIT
    block = lax.axis_index("col")
    y = (lax.axis_index("row").astype(jnp.int32) // shared).reshape(1)

    packed = pack(y, col_values)
    packed = lax.all_to_all(packed, "col", split_axis=0, concat_axis=0, tiled=True)

    arrived, tiles = [], []
    for d in range(1, SPLIT):
        pairs = [(i, (i + d * shared) % row_size) for i in range(row_size)]
        arrived.append(lax.ppermute(slab_values, "row", pairs))
        tiles.append(lax.ppermute(slab_tile, "row", pairs))

    own = make_terms(y, primal, dual_inv, [slab_tile], [slab_values])
    rest = make_terms(y, primal, dual_inv, tiles, arrived)
    parts = contract(packed, own, rest, row_size)
    parts = lax.all_to_all(parts, "row", split_axis=0, concat_axis=0, tiled=True)
    perm = lax.dynamic_slice_in_dim(col_perm, block, 1, axis=0)
    placed = place(perm, parts)
    placed = lax.all_to_all(placed, "col", split_axis=0, concat_axis=0, tiled=True)
    return jnp.sum(placed, axis=0)


def solution(mesh):
    return jax.shard_map(
        functools.partial(body, mesh.shape["row"]),
        mesh=mesh,
        in_specs=(
            P("col", None, None),
            P("col", None, None),
            P(None, None, "col", None),
            P(),
            P("col", "row", None),
            P("col", "row"),
        ),
        out_specs=P("row", "col"),
        check_vma=False,
    )
```

```python
import functools

import jax
import jax.numpy as jnp
from jax import lax
from jax.experimental import pallas as pl
from jax.experimental.pallas import tpu as pltpu
from jax.sharding import PartitionSpec as P

TILE = 64
HALF = TILE // 2
LANES = 128
PACKED = TILE * HALF + LANES
SPLIT = 4
F32 = jnp.float32
BF16 = jnp.bfloat16


def lane_parts(shape, first_vreg):
    lane = lax.broadcasted_iota(jnp.int32, shape, len(shape) - 1)
    e = lane // TILE + 2 * first_vreg
    h = (lane % TILE) // HALF
    f = lane % HALF
    return e, h, f


def pack_kernel(y_ref, values_ref, out_ref):
    blocks, groups, rows, width = values_ref.shape
    half = width // 2
    count = blocks * groups * rows
    for j in range(half // LANES):
        lanes = slice(j * LANES, (j + 1) * LANES)
        e, h, f = lane_parts((count, LANES), j)
        upper = values_ref[:, :, :, lanes].astype(F32).reshape(count, LANES)
        lower = values_ref[:, :, :, half + j * LANES : half + (j + 1) * LANES].astype(F32).reshape(count, LANES)
        lower = pltpu.roll(lower, LANES - HALF, 1)
        kept = jnp.where((h == 1) | (e <= f), upper, lower)
        extra = jnp.where((h == 0) & (e == f), lower, 0.0 if j == 0 else extra)
        out_ref[:, :, :, lanes] = kept.reshape(blocks, groups, rows, LANES).astype(BF16)
    out_ref[:, :, :, half:] = extra.reshape(blocks, groups, rows, LANES).astype(BF16)


def pack(y, values):
    blocks, tiles, rows, width = values.shape
    groups = tiles // SPLIT
    step = blocks // 2
    return pl.pallas_call(
        pack_kernel,
        out_shape=jax.ShapeDtypeStruct((blocks, groups, rows, PACKED), BF16),
        grid_spec=pltpu.PrefetchScalarGridSpec(
            num_scalar_prefetch=1,
            grid=(blocks // step,),
            in_specs=[pl.BlockSpec((step, groups, rows, width), lambda g, y: (g, y[0], 0, 0))],
            out_specs=pl.BlockSpec((step, groups, rows, PACKED), lambda g, y: (g, 0, 0, 0)),
        ),
        compiler_params=pltpu.CompilerParams(vmem_limit_bytes=59 << 20),
        cost_estimate=pl.CostEstimate(flops=10**7, transcendentals=0, bytes_accessed=7 * 10**6),
        name="pack",
    )(y, values)


def split2(x):
    high = x.astype(BF16)
    low = (x - high.astype(F32)).astype(BF16)
    return high, low


ROWS = 16
EXTRA = 16


def terms_kernel(parts, y_ref, primal_ref, dual_ref, *refs):
    slabs, tile_rows = refs[:parts], refs[parts : 2 * parts]
    out_ref, dual_w, primal_w, stage, weights, terms, tile_rows_i, tile_ids = refs[2 * parts :]
    tiles = dual_w.shape[0]
    groups = out_ref.shape[0]
    step = pl.program_id(0)
    steps = pl.num_programs(0) // len(slabs)
    low_lanes = lax.broadcasted_iota(jnp.int32, (HALF, LANES), 1) < TILE

    @pl.when(step == 0)
    def prepare():
        for k in range(parts):
            tile_rows_i[k] = tile_rows[k][...].astype(F32).astype(jnp.int32)[:8]
        pltpu.sync_copy(tile_rows_i, tile_ids)
        for t in range(tiles):
            high, low = split2(dual_ref[0, t * TILE : (t + 1) * TILE, :])
            dual_w[t, :TILE, :] = high
            dual_w[t, TILE:, :] = low
        source = lax.broadcasted_iota(jnp.int32, (LANES, 2 * LANES), 0)
        target = lax.broadcasted_iota(jnp.int32, (LANES, 2 * LANES), 1)
        wanted = (target // LANES) * TILE + 2 * (target % HALF) + (target % TILE) // HALF
        spread = jnp.where(source == wanted, 1.0, 0.0).astype(BF16)
        for j in range(tiles // 2):
            stage[...] = primal_ref[0, :, j * LANES : (j + 1) * LANES]
            x = jnp.concatenate(
                [
                    stage[pl.ds(u * TILE + par, HALF, stride=2), :]
                    for u in range(groups)
                    for par in range(2)
                ],
                axis=0,
            )
            for place, part in enumerate(split2(x)):
                part = jnp.dot(part, spread, preferred_element_type=F32).astype(BF16)
                lanes = slice(place * LANES, (place + 1) * LANES)
                primal_w[2 * j, :, lanes] = part[:, :LANES]
                primal_w[2 * j + 1, :, lanes] = part[:, LANES:]

    for k, slab_ref in enumerate(slabs):

        @pl.when(step // steps == k)
        def spread_rows():
            for m in range(HALF):
                terms[0, pl.ds(m, ROWS, stride=HALF), :] = slab_ref[:, m * LANES : (m + 1) * LANES].astype(F32)

    tile_of = [tile_ids[step // steps, 0, (step % steps) * ROWS + i] for i in range(ROWS)]

    for i in range(ROWS):
        z = terms[0, i * HALF : (i + 1) * HALF, :]
        turned = pltpu.roll(z, TILE, 1)
        square = jnp.concatenate(
            [
                jnp.where(low_lanes, z, turned).astype(BF16),
                jnp.where(low_lanes, turned, z).astype(BF16),
            ],
            axis=0,
        )
        panel = jnp.dot(square, dual_w[tile_of[i]], preferred_element_type=F32)
        high, low = split2(panel)
        weights[i, :TILE, :] = high
        weights[i, TILE:, :] = low

    for i in range(ROWS):
        t = tile_of[i]
        for pair in range(groups // 2):
            lanes = slice(pair * LANES, (pair + 1) * LANES)
            right = weights[i, :, lanes]
            out = jnp.dot(
                primal_w[t, pair * LANES : (pair + 1) * LANES, :],
                jnp.concatenate([right, right], axis=0),
                preferred_element_type=F32,
            )
            even0, odd0, even1, odd1 = (out[q * HALF : (q + 1) * HALF] for q in range(4))
            mixed = pltpu.roll(jnp.where(low_lanes, odd0, even1), TILE, 1)
            terms[2 * pair, pl.ds(i, HALF, stride=ROWS), :] = jnp.where(low_lanes, even0, mixed)
            terms[2 * pair + 1, pl.ds(i, HALF, stride=ROWS), :] = jnp.where(low_lanes, mixed, odd1)

    for u in range(groups):
        for m in range(HALF):
            out_ref[u, :, m * LANES : (m + 1) * LANES] = terms[u, m * ROWS : (m + 1) * ROWS, :].astype(BF16)


def make_terms(y, primal, dual, *slabs):
    order = primal.shape[1]
    tiles = order // TILE
    groups = tiles // SPLIT
    count = slabs[0].shape[0] - EXTRA
    steps = count // ROWS
    width = groups * TILE
    total = count * len(slabs)

    def slab_spec(k):
        return pl.BlockSpec(
            (ROWS, TILE * TILE),
            lambda g, y: (jnp.clip(g - k * steps, 0, steps - 1), 0),
        )

    return pl.pallas_call(
        functools.partial(terms_kernel, len(slabs)),
        out_shape=jax.ShapeDtypeStruct((groups, total, TILE * TILE), BF16),
        grid_spec=pltpu.PrefetchScalarGridSpec(
            num_scalar_prefetch=1,
            grid=(total // ROWS,),
            in_specs=[
                pl.BlockSpec((1, width, order), lambda g, y: (0, y[0], 0)),
                pl.BlockSpec((1, order, width), lambda g, y: (0, 0, y[0])),
                *(slab_spec(k) for k in range(len(slabs))),
                *(pl.BlockSpec((EXTRA, LANES), lambda g, y: (count // EXTRA, 0)) for _ in slabs),
            ],
            out_specs=pl.BlockSpec((groups, ROWS, TILE * TILE), lambda g, y: (0, g, 0)),
            scratch_shapes=[
                pltpu.VMEM((tiles, 2 * TILE, width), BF16),
                pltpu.VMEM((tiles, width, 4 * TILE), BF16),
                pltpu.VMEM((width, LANES), F32),
                pltpu.VMEM((ROWS, 2 * TILE, width), BF16),
                pltpu.VMEM((groups, HALF * ROWS, LANES), F32),
                pltpu.VMEM((len(slabs), 8, LANES), jnp.int32),
                pltpu.SMEM((len(slabs), 8, LANES), jnp.int32),
            ],
        ),
        compiler_params=pltpu.CompilerParams(vmem_limit_bytes=61 << 20),
        cost_estimate=pl.CostEstimate(
            flops=total * 10**8, transcendentals=0, bytes_accessed=2 * 10**6 + total * 40000
        ),
        name="terms",
    )(y, primal, dual, *slabs, *slabs)


STEP = 256


def contract_kernel(packed_ref, own_ref, rest_ref, out_ref, turned, weights):
    group = pl.program_id(0)
    count, _, small, _ = packed_ref.shape
    targets, sources, _ = out_ref.shape
    for v in range(PACKED // LANES):
        lanes = slice(v * LANES, (v + 1) * LANES)
        part = packed_ref[:, 0, :, lanes].astype(F32).reshape(count * small, LANES)
        turned[lanes, :] = part.T
    place = lax.broadcasted_iota(jnp.int32, (HALF, LANES), 0)
    for e in range(HALF):
        mixed = turned[e * TILE : e * TILE + HALF, :]
        square = turned[e * TILE + HALF : (e + 1) * TILE, :]
        mixed_t = turned[pl.ds(e, HALF, stride=TILE), :]
        square_t = turned[pl.ds(HALF + e, HALF, stride=TILE), :]
        start = TILE * HALF + (e % 2) * TILE + e
        diagonal = turned[start : start + 1, :]
        first = jnp.where(place >= e, mixed, mixed_t)
        last = jnp.where(place == e, diagonal, jnp.where(place < e, mixed, mixed_t))
        up = jnp.concatenate([first, square], axis=0)
        low = jnp.concatenate([square_t, last], axis=0)
        weights[e * TILE : (e + 1) * TILE, :] = up.astype(BF16)
        weights[(HALF + e) * TILE : (HALF + e + 1) * TILE, :] = low.astype(BF16)
    left = jnp.concatenate([own_ref[0], rest_ref[0]], axis=0)
    acc = jnp.dot(left, weights[...], preferred_element_type=F32)
    for s in range(sources // 8):
        for r in range(targets):
            start = (s * targets + r) * 8
            out_ref[r, s * 8 : (s + 1) * 8, :] = acc[start : start + 8, :]


def contract(packed, own, rest, targets):
    count, groups, small, _ = packed.shape
    _, own_rows, width = own.shape
    rest_rows = rest.shape[1]
    total = own_rows + rest_rows
    return pl.pallas_call(
        contract_kernel,
        out_shape=jax.ShapeDtypeStruct((targets, total // targets, groups * LANES), F32),
        grid_spec=pltpu.PrefetchScalarGridSpec(
            num_scalar_prefetch=0,
            grid=(groups,),
            in_specs=[
                pl.BlockSpec((count, 1, small, PACKED), lambda g: (0, g, 0, 0)),
                pl.BlockSpec((1, own_rows, width), lambda g: (g, 0, 0)),
                pl.BlockSpec((1, rest_rows, width), lambda g: (g, 0, 0)),
            ],
            out_specs=pl.BlockSpec((targets, total // targets, LANES), lambda g: (0, 0, g)),
            scratch_shapes=[
                pltpu.VMEM((PACKED, LANES), F32),
                pltpu.VMEM((width, LANES), BF16),
            ],
        ),
        compiler_params=pltpu.CompilerParams(vmem_limit_bytes=59 << 20),
        cost_estimate=pl.CostEstimate(flops=6 * 10**9, transcendentals=0, bytes_accessed=2 * 10**7),
        name="contract",
    )(packed, own, rest)


def place_kernel(perm_ref, parts_ref, out_ref, left):
    step = pl.program_id(0)
    sources, rows, width = parts_ref.shape
    total = sources * 8

    @pl.when(step == 0)
    def prepare():
        for y_s in range(SPLIT):
            for z in range(sources // SPLIT):
                for y in range(SPLIT):
                    d = (y_s - y) % SPLIT
                    value = parts_ref[y_s * (sources // SPLIT) + z, d * 8 : (d + 1) * 8, :]
                    start = (y * (sources // SPLIT) + z) * 8
                    left[start : start + 8, y_s * width : (y_s + 1) * width] = value

    value = left[...]
    high = value.astype(BF16)
    value = value - high.astype(F32)
    middle = value.astype(BF16)
    low = (value - middle.astype(F32)).astype(BF16)
    pieces = jnp.concatenate([high, middle, low], axis=0)
    target = lax.broadcasted_iota(jnp.int32, (STEP, perm_ref.shape[1]), 0) + step * STEP
    chosen = jnp.where(perm_ref[...] == target, 1.0, 0.0).astype(BF16)
    out = lax.dot_general(pieces, chosen, (((1,), (1,)), ((), ())), preferred_element_type=F32)
    out = out[:total] + out[total : 2 * total] + out[2 * total :]
    for c in range(STEP // LANES):
        out_ref[c] = out[:, c * LANES : (c + 1) * LANES]


def place(perm, parts):
    sources, rows, width = parts.shape
    columns = perm.shape[1]
    total = sources * 8
    return pl.pallas_call(
        place_kernel,
        out_shape=jax.ShapeDtypeStruct((columns // LANES, total, LANES), F32),
        grid_spec=pltpu.PrefetchScalarGridSpec(
            num_scalar_prefetch=0,
            grid=(columns // STEP,),
            in_specs=[
                pl.BlockSpec((1, columns), lambda g: (0, 0)),
                pl.BlockSpec((sources, rows, width), lambda g: (0, 0, 0)),
            ],
            out_specs=pl.BlockSpec((STEP // LANES, total, LANES), lambda g: (g, 0, 0)),
            scratch_shapes=[pltpu.VMEM((total, columns), F32)],
        ),
        compiler_params=pltpu.CompilerParams(vmem_limit_bytes=40 << 20),
        cost_estimate=pl.CostEstimate(flops=2 * 10**9, transcendentals=0, bytes_accessed=10**6),
        name="place",
    )(perm, parts)


def body(row_size, primal, dual_inv, col_values, col_perm, slab_values, slab_tile):
    count = slab_values.shape[1]
    shared = row_size // SPLIT
    block = lax.axis_index("col")
    y = (lax.axis_index("row").astype(jnp.int32) // shared).reshape(1)

    packed = pack(y, col_values)
    packed = lax.all_to_all(packed, "col", split_axis=0, concat_axis=0, tiled=True)

    tile_row = jnp.pad(slab_tile.astype(BF16), ((0, EXTRA - 1), (0, TILE * TILE - count)))
    message = jnp.concatenate([slab_values[0], tile_row], axis=0)
    arrived = []
    for d in range(1, SPLIT):
        pairs = [(i, (i + d * shared) % row_size) for i in range(row_size)]
        arrived.append(lax.ppermute(message, "row", pairs))

    own = make_terms(y, primal, dual_inv, message)
    rest = make_terms(y, primal, dual_inv, *arrived)
    parts = contract(packed, own, rest, row_size)
    parts = lax.all_to_all(parts, "row", split_axis=0, concat_axis=0, tiled=True)
    perm = lax.dynamic_slice_in_dim(col_perm, block, 1, axis=0)
    placed = place(perm, parts)
    placed = lax.all_to_all(placed, "col", split_axis=0, concat_axis=0, tiled=True)
    return jnp.sum(placed, axis=0)


def solution(mesh):
    return jax.shard_map(
        functools.partial(body, mesh.shape["row"]),
        mesh=mesh,
        in_specs=(
            P("col", None, None),
            P("col", None, None),
            P(None, None, "col", None),
            P(),
            P("col", "row", None),
            P("col", "row"),
        ),
        out_specs=P("row", "col"),
        check_vma=False,
    )
```

```python
import functools

import jax
import jax.numpy as jnp
from jax import lax
from jax.experimental import pallas as pl
from jax.experimental.pallas import tpu as pltpu
from jax.sharding import PartitionSpec as P

TILE = 64
HALF = TILE // 2
LANES = 128
PACKED = TILE * HALF + LANES
SPLIT = 4
F32 = jnp.float32
BF16 = jnp.bfloat16


def lane_parts(shape, first_vreg):
    lane = lax.broadcasted_iota(jnp.int32, shape, len(shape) - 1)
    e = lane // TILE + 2 * first_vreg
    h = (lane % TILE) // HALF
    f = lane % HALF
    return e, h, f


def pack_kernel(y_ref, values_ref, out_ref):
    blocks, groups, rows, width = values_ref.shape
    half = width // 2
    count = blocks * groups * rows
    for j in range(half // LANES):
        lanes = slice(j * LANES, (j + 1) * LANES)
        e, h, f = lane_parts((count, LANES), j)
        upper = values_ref[:, :, :, lanes].astype(F32).reshape(count, LANES)
        lower = values_ref[:, :, :, half + j * LANES : half + (j + 1) * LANES].astype(F32).reshape(count, LANES)
        lower = pltpu.roll(lower, LANES - HALF, 1)
        kept = jnp.where((h == 1) | (e <= f), upper, lower)
        extra = jnp.where((h == 0) & (e == f), lower, 0.0 if j == 0 else extra)
        out_ref[:, :, :, lanes] = kept.reshape(blocks, groups, rows, LANES).astype(BF16)
    out_ref[:, :, :, half:] = extra.reshape(blocks, groups, rows, LANES).astype(BF16)


def pack(y, values):
    blocks, tiles, rows, width = values.shape
    groups = tiles // SPLIT
    step = blocks // 2
    return pl.pallas_call(
        pack_kernel,
        out_shape=jax.ShapeDtypeStruct((blocks, groups, rows, PACKED), BF16),
        grid_spec=pltpu.PrefetchScalarGridSpec(
            num_scalar_prefetch=1,
            grid=(blocks // step,),
            in_specs=[pl.BlockSpec((step, groups, rows, width), lambda g, y: (g, y[0], 0, 0))],
            out_specs=pl.BlockSpec((step, groups, rows, PACKED), lambda g, y: (g, 0, 0, 0)),
        ),
        compiler_params=pltpu.CompilerParams(vmem_limit_bytes=59 << 20),
        cost_estimate=pl.CostEstimate(flops=10**7, transcendentals=0, bytes_accessed=7 * 10**6),
        name="pack",
    )(y, values)


def pack_slab_kernel(slab_ref, tile_ref, out_ref):
    half = slab_ref.shape[2] // 2
    count = slab_ref.shape[1]
    extra = jnp.zeros((count, LANES), F32)
    for j in range(half // LANES):
        e, h, f = lane_parts((count, LANES), j)
        upper = slab_ref[0, :, j * LANES : (j + 1) * LANES].astype(F32)
        lower = slab_ref[0, :, half + j * LANES : half + (j + 1) * LANES].astype(F32)
        lower = pltpu.roll(lower, LANES - HALF, 1)
        kept = jnp.where((h == 1) | (e <= f), upper, lower)
        extra = jnp.where((h == 0) & (e == f), lower, extra)
        out_ref[:, j * LANES : (j + 1) * LANES] = kept.astype(BF16)
    ids = tile_ref[...].astype(F32)
    ids = jnp.concatenate([jnp.zeros((1, LANES - count), F32), ids], axis=1)
    lane = lax.broadcasted_iota(jnp.int32, (count, LANES), 1)
    extra = extra + jnp.where(lane < TILE, pltpu.roll(extra, TILE, 1), 0.0)
    out_ref[:, half:] = jnp.where(lane < TILE, extra, ids).astype(BF16)


def pack_slab(slab, tile_of):
    _, count, width = slab.shape
    return pl.pallas_call(
        pack_slab_kernel,
        out_shape=jax.ShapeDtypeStruct((count, PACKED), BF16),
        cost_estimate=pl.CostEstimate(flops=10**6, transcendentals=0, bytes_accessed=10**6),
        name="pack_slab",
    )(slab, tile_of)


def split2(x):
    high = x.astype(BF16)
    low = (x - high.astype(F32)).astype(BF16)
    return high, low


ROWS = 16
EXTRA = 16


def terms_kernel(parts, y_ref, primal_ref, dual_ref, *refs):
    slabs, tile_rows = refs[:parts], refs[parts : 2 * parts]
    out_ref, dual_w, primal_w, stage, weights, terms, diagonals, tile_rows_i, tile_ids = refs[2 * parts :]
    tiles = dual_w.shape[0]
    groups = out_ref.shape[0]
    step = pl.program_id(0)
    steps = pl.num_programs(0) // len(slabs)
    lane_i = lax.broadcasted_iota(jnp.int32, (HALF, LANES), 1)
    row_i = lax.broadcasted_iota(jnp.int32, (HALF, LANES), 0)
    lane_i2 = lax.broadcasted_iota(jnp.int32, (TILE, LANES), 1)
    low_lanes = lane_i < TILE

    @pl.when(step == 0)
    def prepare():
        for k in range(parts):
            tile_rows_i[k] = tile_rows[k][...].astype(F32).astype(jnp.int32)[:8]
        pltpu.sync_copy(tile_rows_i, tile_ids)
        for t in range(tiles):
            high, low = split2(dual_ref[0, t * TILE : (t + 1) * TILE, :])
            dual_w[t, :TILE, :] = high
            dual_w[t, TILE:, :] = low
        source = lax.broadcasted_iota(jnp.int32, (LANES, 2 * LANES), 0)
        target = lax.broadcasted_iota(jnp.int32, (LANES, 2 * LANES), 1)
        wanted = (target // LANES) * TILE + target % TILE
        spread = jnp.where(source == wanted, 1.0, 0.0).astype(BF16)
        for j in range(tiles // 2):
            stage[...] = primal_ref[0, :, j * LANES : (j + 1) * LANES]
            x = jnp.concatenate(
                [
                    stage[pl.ds(u * TILE + par, HALF, stride=2), :]
                    for u in range(groups)
                    for par in range(2)
                ],
                axis=0,
            )
            for place, part in enumerate(split2(x)):
                part = jnp.dot(part, spread, preferred_element_type=F32).astype(BF16)
                lanes = slice(place * LANES, (place + 1) * LANES)
                primal_w[2 * j, :, lanes] = part[:, :LANES]
                primal_w[2 * j + 1, :, lanes] = part[:, LANES:]

    for k, slab_ref in enumerate(slabs):

        @pl.when(step // steps == k)
        def spread_rows():
            for m in range(HALF // 2):
                part = slab_ref[:, m * LANES : (m + 1) * LANES].astype(F32)
                terms[0, pl.ds(2 * m, ROWS, stride=HALF), :] = part
                terms[0, pl.ds(2 * m + 1, ROWS, stride=HALF), :] = pltpu.roll(part, TILE, 1)
            diagonals[...] = slab_ref[:, TILE * HALF :].astype(F32)

    tile_of = [tile_ids[step // steps, 0, TILE + (step % steps) * ROWS + i] for i in range(ROWS)]

    for i in range(ROWS):
        z = terms[0, i * HALF : (i + 1) * HALF, :]
        turned = z.T
        z_t = jnp.concatenate([turned[:HALF], jnp.zeros((HALF, LANES - HALF), F32)], axis=1)
        square_t = jnp.concatenate([turned[HALF:TILE], jnp.zeros((HALF, LANES - HALF), F32)], axis=1)
        top = jnp.where(lane_i >= row_i, z, z_t)
        corner = jnp.where(lane_i < row_i, z, z_t)
        corner = jnp.where(lane_i == row_i, diagonals[i : i + 1, :], corner)
        bottom = jnp.where(lane_i < HALF, square_t, pltpu.roll(corner, HALF, 1))
        square = jnp.concatenate([top, bottom], axis=0)
        square = jnp.where(lane_i2 < TILE, square, pltpu.roll(square, TILE, 1)).astype(BF16)
        panel = jnp.dot(square, dual_w[tile_of[i]], preferred_element_type=F32)
        high, low = split2(panel)
        weights[i, :TILE, :] = high
        weights[i, TILE:, :] = low

    for i in range(ROWS):
        t = tile_of[i]
        right = weights[i]
        product = jnp.dot(primal_w[t], jnp.concatenate([right, right], axis=0), preferred_element_type=F32)
        for pair in range(groups // 2):
            lanes = slice(pair * LANES, (pair + 1) * LANES)
            out = product[pair * LANES : (pair + 1) * LANES, lanes]
            even0, odd0, even1, odd1 = (out[q * HALF : (q + 1) * HALF] for q in range(4))
            mixed = pltpu.roll(jnp.where(low_lanes, odd0, even1), TILE, 1)
            terms[2 * pair, pl.ds(i, HALF, stride=ROWS), :] = jnp.where(low_lanes, even0, mixed)
            terms[2 * pair + 1, pl.ds(i, HALF, stride=ROWS), :] = jnp.where(low_lanes, mixed, odd1)

    for u in range(groups):
        for m in range(HALF):
            out_ref[u, :, m * LANES : (m + 1) * LANES] = terms[u, m * ROWS : (m + 1) * ROWS, :].astype(BF16)


def make_terms(y, primal, dual, *slabs):
    order = primal.shape[1]
    tiles = order // TILE
    groups = tiles // SPLIT
    count = slabs[0].shape[0]
    steps = count // ROWS
    width = groups * TILE
    total = count * len(slabs)

    def slab_spec(k):
        return pl.BlockSpec(
            (ROWS, PACKED),
            lambda g, y: (jnp.clip(g - k * steps, 0, steps - 1), 0),
        )

    return pl.pallas_call(
        functools.partial(terms_kernel, len(slabs)),
        out_shape=jax.ShapeDtypeStruct((groups, total, TILE * TILE), BF16),
        grid_spec=pltpu.PrefetchScalarGridSpec(
            num_scalar_prefetch=1,
            grid=(total // ROWS,),
            in_specs=[
                pl.BlockSpec((1, width, order), lambda g, y: (0, y[0], 0)),
                pl.BlockSpec((1, order, width), lambda g, y: (0, 0, y[0])),
                *(slab_spec(k) for k in range(len(slabs))),
                *(pl.BlockSpec((EXTRA, LANES), lambda g, y: (0, TILE * HALF // LANES)) for _ in slabs),
            ],
            out_specs=pl.BlockSpec((groups, ROWS, TILE * TILE), lambda g, y: (0, g, 0)),
            scratch_shapes=[
                pltpu.VMEM((tiles, 2 * TILE, width), BF16),
                pltpu.VMEM((tiles, width, 4 * TILE), BF16),
                pltpu.VMEM((width, LANES), F32),
                pltpu.VMEM((ROWS, 2 * TILE, width), BF16),
                pltpu.VMEM((groups, HALF * ROWS, LANES), F32),
                pltpu.VMEM((ROWS, LANES), F32),
                pltpu.VMEM((len(slabs), 8, LANES), jnp.int32),
                pltpu.SMEM((len(slabs), 8, LANES), jnp.int32),
            ],
        ),
        compiler_params=pltpu.CompilerParams(vmem_limit_bytes=61 << 20),
        cost_estimate=pl.CostEstimate(
            flops=total * 10**8, transcendentals=0, bytes_accessed=2 * 10**6 + total * 40000
        ),
        name="terms",
    )(y, primal, dual, *slabs, *slabs)


STEP = 256


def contract_kernel(packed_ref, own_ref, rest_ref, out_ref, turned, weights):
    group = pl.program_id(0)
    count, _, small, _ = packed_ref.shape
    targets, sources, _ = out_ref.shape
    for v in range(PACKED // LANES):
        lanes = slice(v * LANES, (v + 1) * LANES)
        part = packed_ref[:, 0, :, lanes].astype(F32).reshape(count * small, LANES)
        turned[lanes, :] = part.T
    place = lax.broadcasted_iota(jnp.int32, (HALF, LANES), 0)
    for e in range(HALF):
        mixed = turned[e * TILE : e * TILE + HALF, :]
        square = turned[e * TILE + HALF : (e + 1) * TILE, :]
        mixed_t = turned[pl.ds(e, HALF, stride=TILE), :]
        square_t = turned[pl.ds(HALF + e, HALF, stride=TILE), :]
        start = TILE * HALF + (e % 2) * TILE + e
        diagonal = turned[start : start + 1, :]
        first = jnp.where(place >= e, mixed, mixed_t)
        last = jnp.where(place == e, diagonal, jnp.where(place < e, mixed, mixed_t))
        up = jnp.concatenate([first, square], axis=0)
        low = jnp.concatenate([square_t, last], axis=0)
        weights[e * TILE : (e + 1) * TILE, :] = up.astype(BF16)
        weights[(HALF + e) * TILE : (HALF + e + 1) * TILE, :] = low.astype(BF16)
    left = jnp.concatenate([own_ref[0], rest_ref[0]], axis=0)
    acc = jnp.dot(left, weights[...], preferred_element_type=F32)
    for s in range(sources // 8):
        for r in range(targets):
            start = (s * targets + r) * 8
            out_ref[r, s * 8 : (s + 1) * 8, :] = acc[start : start + 8, :]


def contract(packed, own, rest, targets):
    count, groups, small, _ = packed.shape
    _, own_rows, width = own.shape
    rest_rows = rest.shape[1]
    total = own_rows + rest_rows
    return pl.pallas_call(
        contract_kernel,
        out_shape=jax.ShapeDtypeStruct((targets, total // targets, groups * LANES), F32),
        grid_spec=pltpu.PrefetchScalarGridSpec(
            num_scalar_prefetch=0,
            grid=(groups,),
            in_specs=[
                pl.BlockSpec((count, 1, small, PACKED), lambda g: (0, g, 0, 0)),
                pl.BlockSpec((1, own_rows, width), lambda g: (g, 0, 0)),
                pl.BlockSpec((1, rest_rows, width), lambda g: (g, 0, 0)),
            ],
            out_specs=pl.BlockSpec((targets, total // targets, LANES), lambda g: (0, 0, g)),
            scratch_shapes=[
                pltpu.VMEM((PACKED, LANES), F32),
                pltpu.VMEM((width, LANES), BF16),
            ],
        ),
        compiler_params=pltpu.CompilerParams(vmem_limit_bytes=59 << 20),
        cost_estimate=pl.CostEstimate(flops=6 * 10**9, transcendentals=0, bytes_accessed=2 * 10**7),
        name="contract",
    )(packed, own, rest)


def place_kernel(perm_ref, parts_ref, out_ref, left):
    step = pl.program_id(0)
    sources, rows, width = parts_ref.shape
    total = sources * 8

    @pl.when(step == 0)
    def prepare():
        for y_s in range(SPLIT):
            for z in range(sources // SPLIT):
                for y in range(SPLIT):
                    d = (y_s - y) % SPLIT
                    value = parts_ref[y_s * (sources // SPLIT) + z, d * 8 : (d + 1) * 8, :]
                    start = (y * (sources // SPLIT) + z) * 8
                    left[start : start + 8, y_s * width : (y_s + 1) * width] = value

    value = left[...]
    high = value.astype(BF16)
    value = value - high.astype(F32)
    middle = value.astype(BF16)
    low = (value - middle.astype(F32)).astype(BF16)
    pieces = jnp.concatenate([high, middle, low], axis=0)
    target = lax.broadcasted_iota(jnp.int32, (STEP, perm_ref.shape[1]), 0) + step * STEP
    chosen = jnp.where(perm_ref[...] == target, 1.0, 0.0).astype(BF16)
    out = lax.dot_general(pieces, chosen, (((1,), (1,)), ((), ())), preferred_element_type=F32)
    out = out[:total] + out[total : 2 * total] + out[2 * total :]
    for c in range(STEP // LANES):
        out_ref[c] = out[:, c * LANES : (c + 1) * LANES]


def place(perm, parts):
    sources, rows, width = parts.shape
    columns = perm.shape[1]
    total = sources * 8
    return pl.pallas_call(
        place_kernel,
        out_shape=jax.ShapeDtypeStruct((columns // LANES, total, LANES), F32),
        grid_spec=pltpu.PrefetchScalarGridSpec(
            num_scalar_prefetch=0,
            grid=(columns // STEP,),
            in_specs=[
                pl.BlockSpec((1, columns), lambda g: (0, 0)),
                pl.BlockSpec((sources, rows, width), lambda g: (0, 0, 0)),
            ],
            out_specs=pl.BlockSpec((STEP // LANES, total, LANES), lambda g: (g, 0, 0)),
            scratch_shapes=[pltpu.VMEM((total, columns), F32)],
        ),
        compiler_params=pltpu.CompilerParams(vmem_limit_bytes=40 << 20),
        cost_estimate=pl.CostEstimate(flops=2 * 10**9, transcendentals=0, bytes_accessed=10**6),
        name="place",
    )(perm, parts)


def body(row_size, primal, dual_inv, col_values, col_perm, slab_values, slab_tile):
    count = slab_values.shape[1]
    shared = row_size // SPLIT
    block = lax.axis_index("col")
    y = (lax.axis_index("row").astype(jnp.int32) // shared).reshape(1)

    packed = pack(y, col_values)
    packed = lax.all_to_all(packed, "col", split_axis=0, concat_axis=0, tiled=True)

    message = pack_slab(slab_values, slab_tile)
    arrived = []
    for d in range(1, SPLIT):
        pairs = [(i, (i + d * shared) % row_size) for i in range(row_size)]
        arrived.append(lax.ppermute(message, "row", pairs))

    own = make_terms(y, primal, dual_inv, message)
    rest = make_terms(y, primal, dual_inv, *arrived)
    parts = contract(packed, own, rest, row_size)
    parts = lax.all_to_all(parts, "row", split_axis=0, concat_axis=0, tiled=True)
    perm = lax.dynamic_slice_in_dim(col_perm, block, 1, axis=0)
    placed = place(perm, parts)
    placed = lax.all_to_all(placed, "col", split_axis=0, concat_axis=0, tiled=True)
    return jnp.sum(placed, axis=0)


def solution(mesh):
    return jax.shard_map(
        functools.partial(body, mesh.shape["row"]),
        mesh=mesh,
        in_specs=(
            P("col", None, None),
            P("col", None, None),
            P(None, None, "col", None),
            P(),
            P("col", "row", None),
            P("col", "row"),
        ),
        out_specs=P("row", "col"),
        check_vma=False,
    )
```

```python
import functools

import jax
import jax.numpy as jnp
from jax import lax
from jax.experimental import pallas as pl
from jax.experimental.pallas import tpu as pltpu
from jax.sharding import PartitionSpec as P

TILE = 64
HALF = TILE // 2
LANES = 128
PACKED = TILE * HALF + LANES
SPLIT = 4
F32 = jnp.float32
BF16 = jnp.bfloat16


def lane_parts(shape, first_vreg):
    lane = lax.broadcasted_iota(jnp.int32, shape, len(shape) - 1)
    e = lane // TILE + 2 * first_vreg
    h = (lane % TILE) // HALF
    f = lane % HALF
    return e, h, f


def pack_kernel(y_ref, values_ref, out_ref):
    blocks, groups, rows, width = values_ref.shape
    half = width // 2
    count = blocks * groups * rows
    for j in range(half // LANES):
        lanes = slice(j * LANES, (j + 1) * LANES)
        e, h, f = lane_parts((count, LANES), j)
        upper = values_ref[:, :, :, lanes].astype(F32).reshape(count, LANES)
        lower = values_ref[:, :, :, half + j * LANES : half + (j + 1) * LANES].astype(F32).reshape(count, LANES)
        lower = pltpu.roll(lower, LANES - HALF, 1)
        kept = jnp.where((h == 1) | (e <= f), upper, lower)
        extra = jnp.where((h == 0) & (e == f), lower, 0.0 if j == 0 else extra)
        out_ref[:, :, :, lanes] = kept.reshape(blocks, groups, rows, LANES).astype(BF16)
    out_ref[:, :, :, half:] = extra.reshape(blocks, groups, rows, LANES).astype(BF16)


def pack(y, values):
    blocks, tiles, rows, width = values.shape
    groups = tiles // SPLIT
    step = blocks // 2
    return pl.pallas_call(
        pack_kernel,
        out_shape=jax.ShapeDtypeStruct((blocks, groups, rows, PACKED), BF16),
        grid_spec=pltpu.PrefetchScalarGridSpec(
            num_scalar_prefetch=1,
            grid=(blocks // step,),
            in_specs=[pl.BlockSpec((step, groups, rows, width), lambda g, y: (g, y[0], 0, 0))],
            out_specs=pl.BlockSpec((step, groups, rows, PACKED), lambda g, y: (g, 0, 0, 0)),
        ),
        compiler_params=pltpu.CompilerParams(vmem_limit_bytes=59 << 20),
        cost_estimate=pl.CostEstimate(flops=10**7, transcendentals=0, bytes_accessed=7 * 10**6),
        name="pack",
    )(y, values)


def pack_slab_kernel(slab_ref, tile_ref, out_ref):
    half = slab_ref.shape[2] // 2
    count = slab_ref.shape[1]
    extra = jnp.zeros((count, LANES), F32)
    for j in range(half // LANES):
        e, h, f = lane_parts((count, LANES), j)
        upper = slab_ref[0, :, j * LANES : (j + 1) * LANES].astype(F32)
        lower = slab_ref[0, :, half + j * LANES : half + (j + 1) * LANES].astype(F32)
        lower = pltpu.roll(lower, LANES - HALF, 1)
        kept = jnp.where((h == 1) | (e <= f), upper, lower)
        extra = jnp.where((h == 0) & (e == f), lower, extra)
        out_ref[:, j * LANES : (j + 1) * LANES] = kept.astype(BF16)
    ids = tile_ref[...].astype(F32)
    ids = jnp.concatenate([jnp.zeros((1, LANES - count), F32), ids], axis=1)
    lane = lax.broadcasted_iota(jnp.int32, (count, LANES), 1)
    extra = extra + jnp.where(lane < TILE, pltpu.roll(extra, TILE, 1), 0.0)
    out_ref[:, half:] = jnp.where(lane < TILE, extra, ids).astype(BF16)


def pack_slab(slab, tile_of):
    _, count, width = slab.shape
    return pl.pallas_call(
        pack_slab_kernel,
        out_shape=jax.ShapeDtypeStruct((count, PACKED), BF16),
        cost_estimate=pl.CostEstimate(flops=10**6, transcendentals=0, bytes_accessed=10**6),
        name="pack_slab",
    )(slab, tile_of)


def split2(x):
    high = x.astype(BF16)
    low = (x - high.astype(F32)).astype(BF16)
    return high, low


ROWS = 16
EXTRA = 16
OUT_STRIDE = 24
ROW_STRIDE = 40
TURN_STRIDE = 72


def terms_kernel(parts, ready, y_ref, first_ref, second_ref, *refs):
    slabs, tile_rows, refs = refs[:parts], refs[parts : 2 * parts], refs[2 * parts :]
    if ready:
        dual_w, primal_w = first_ref, second_ref
        out_ref, weights, terms, diagonals, tile_rows_i, tile_ids = refs
    else:
        primal_ref, dual_ref = first_ref, second_ref
        out_ref, dual_w, primal_w, weights, terms, diagonals, tile_rows_i, tile_ids, stage = refs
    tiles = dual_w.shape[0]
    groups = out_ref.shape[0]
    step = pl.program_id(0)
    steps = pl.num_programs(0) // len(slabs)
    lane_i = lax.broadcasted_iota(jnp.int32, (HALF, LANES), 1)
    row_i = lax.broadcasted_iota(jnp.int32, (HALF, LANES), 0)
    lane_i2 = lax.broadcasted_iota(jnp.int32, (TILE, LANES), 1)
    low_lanes = lane_i < TILE

    @pl.when(step == 0)
    def prepare():
        for k in range(parts):
            tile_rows_i[k] = tile_rows[k][...].astype(F32).astype(jnp.int32)[:8]
        pltpu.sync_copy(tile_rows_i, tile_ids)
        if ready:
            return
        for t in range(tiles):
            high, low = split2(dual_ref[0, t * TILE : (t + 1) * TILE, :])
            dual_w[t, :TILE, :] = high
            dual_w[t, TILE:, :] = low
        source = lax.broadcasted_iota(jnp.int32, (LANES, 2 * LANES), 0)
        target = lax.broadcasted_iota(jnp.int32, (LANES, 2 * LANES), 1)
        wanted = (target // LANES) * TILE + target % TILE
        spread = jnp.where(source == wanted, 1.0, 0.0).astype(BF16)
        for j in range(tiles // 2):
            stage[...] = primal_ref[0, :, j * LANES : (j + 1) * LANES]
            x = jnp.concatenate(
                [
                    stage[pl.ds(u * TILE + par, HALF, stride=2), :]
                    for u in range(groups)
                    for par in range(2)
                ],
                axis=0,
            )
            for place, part in enumerate(split2(x)):
                part = jnp.dot(part, spread, preferred_element_type=F32).astype(BF16)
                lanes = slice(place * LANES, (place + 1) * LANES)
                primal_w[2 * j, :, lanes] = part[:, :LANES]
                primal_w[2 * j + 1, :, lanes] = part[:, LANES:]

    for k, slab_ref in enumerate(slabs):

        @pl.when(step // steps == k)
        def spread_rows():
            for m in range(HALF // 2):
                part = slab_ref[:, m * LANES : (m + 1) * LANES].astype(F32)
                terms[0, pl.ds(2 * m, ROWS, stride=ROW_STRIDE), :] = part
                terms[0, pl.ds(2 * m + 1, ROWS, stride=ROW_STRIDE), :] = pltpu.roll(part, TILE, 1)
            diagonals[...] = slab_ref[:, TILE * HALF :].astype(F32)

    tile_of = [tile_ids[step // steps, 0, TILE + (step % steps) * ROWS + i] for i in range(ROWS)]

    for i in range(ROWS):
        z = terms[0, i * ROW_STRIDE : i * ROW_STRIDE + HALF, :]
        turned = z.T
        z_t = jnp.concatenate([turned[:HALF], jnp.zeros((HALF, LANES - HALF), F32)], axis=1)
        square_t = jnp.concatenate([turned[HALF:TILE], jnp.zeros((HALF, LANES - HALF), F32)], axis=1)
        top = jnp.where(lane_i >= row_i, z, z_t)
        corner = jnp.where(lane_i < row_i, z, z_t)
        corner = jnp.where(lane_i == row_i, diagonals[i : i + 1, :], corner)
        bottom = jnp.where(lane_i < HALF, square_t, pltpu.roll(corner, HALF, 1))
        square = jnp.concatenate([top, bottom], axis=0)
        square = jnp.where(lane_i2 < TILE, square, pltpu.roll(square, TILE, 1)).astype(BF16)
        panel = jnp.dot(square, dual_w[tile_of[i]], preferred_element_type=F32)
        high, low = split2(panel)
        weights[i, :TILE, :] = high
        weights[i, TILE:, :] = low

    for i in range(ROWS):
        t = tile_of[i]
        right = weights[i]
        product = jnp.dot(primal_w[t], jnp.concatenate([right, right], axis=0), preferred_element_type=F32)
        for pair in range(groups // 2):
            lanes = slice(pair * LANES, (pair + 1) * LANES)
            out = product[pair * LANES : (pair + 1) * LANES, lanes]
            even0, odd0, even1, odd1 = (out[q * HALF : (q + 1) * HALF] for q in range(4))
            mixed = pltpu.roll(jnp.where(low_lanes, odd0, even1), TILE, 1)
            terms[2 * pair, pl.ds(i, HALF, stride=OUT_STRIDE), :] = jnp.where(low_lanes, even0, mixed)
            terms[2 * pair + 1, pl.ds(i, HALF, stride=OUT_STRIDE), :] = jnp.where(low_lanes, mixed, odd1)

    for u in range(groups):
        for m in range(HALF):
            out_ref[u, :, m * LANES : (m + 1) * LANES] = terms[u, m * OUT_STRIDE : m * OUT_STRIDE + ROWS, :].astype(BF16)


def make_terms(y, matrices, ready, *slabs):
    order = matrices[0].shape[1]
    if ready:
        tiles, _, width = matrices[0].shape
    else:
        tiles = order // TILE
        width = order // SPLIT
    groups = width // TILE
    count = slabs[0].shape[0]
    steps = count // ROWS
    total = count * len(slabs)
    ready_shapes = [(tiles, 2 * TILE, width), (tiles, width, 4 * TILE)]

    def whole(shape):
        return pl.BlockSpec(shape, lambda g, y: (0, 0, 0), pipeline_mode=pl.Buffered(1))

    def slab_spec(k):
        return pl.BlockSpec(
            (ROWS, PACKED),
            lambda g, y: (jnp.clip(g - k * steps, 0, steps - 1), 0),
        )

    if ready:
        matrix_specs = [whole(shape) for shape in ready_shapes]
    else:
        matrix_specs = [
            pl.BlockSpec((1, width, order), lambda g, y: (0, y[0], 0)),
            pl.BlockSpec((1, order, width), lambda g, y: (0, 0, y[0])),
        ]
    out_shape = [jax.ShapeDtypeStruct((groups, total, TILE * TILE), BF16)]
    out_specs = [pl.BlockSpec((groups, ROWS, TILE * TILE), lambda g, y: (0, g, 0))]
    scratch = [
        pltpu.VMEM((ROWS, 2 * TILE, width), BF16),
        pltpu.VMEM((groups, HALF * OUT_STRIDE, LANES), F32),
        pltpu.VMEM((ROWS, LANES), F32),
        pltpu.VMEM((len(slabs), 8, LANES), jnp.int32),
        pltpu.SMEM((len(slabs), 8, LANES), jnp.int32),
    ]
    if not ready:
        out_shape += [jax.ShapeDtypeStruct(shape, BF16) for shape in ready_shapes]
        out_specs += [whole(shape) for shape in ready_shapes]
        scratch += [pltpu.VMEM((width, LANES), F32)]
    return pl.pallas_call(
        functools.partial(terms_kernel, len(slabs), ready),
        out_shape=out_shape,
        grid_spec=pltpu.PrefetchScalarGridSpec(
            num_scalar_prefetch=1,
            grid=(total // ROWS,),
            in_specs=[
                *matrix_specs,
                *(slab_spec(k) for k in range(len(slabs))),
                *(
                    pl.BlockSpec((EXTRA, LANES), lambda g, y: (0, TILE * HALF // LANES))
                    for _ in slabs
                ),
            ],
            out_specs=out_specs,
            scratch_shapes=scratch,
        ),
        compiler_params=pltpu.CompilerParams(vmem_limit_bytes=61 << 20),
        cost_estimate=pl.CostEstimate(
            flops=total * 10**8, transcendentals=0, bytes_accessed=2 * 10**6 + total * 40000
        ),
        name="terms",
    )(y, *matrices, *slabs, *slabs)


STEP = 256


def contract_kernel(packed_ref, own_ref, rest_ref, out_ref, turned, weights):
    group = pl.program_id(0)
    count, _, small, _ = packed_ref.shape
    targets, sources, _ = out_ref.shape
    for v in range(PACKED // LANES):
        lanes = slice(v * LANES, (v + 1) * LANES)
        part = packed_ref[:, 0, :, lanes].astype(F32).reshape(count * small, LANES)
        part = part.T
        if v < HALF // 2:
            for k in range(2):
                turned[(2 * v + k) * TURN_STRIDE : (2 * v + k) * TURN_STRIDE + TILE, :] = part[k * TILE : (k + 1) * TILE]
        else:
            turned[HALF * TURN_STRIDE :, :] = part
    place = lax.broadcasted_iota(jnp.int32, (HALF, LANES), 0)
    for e in range(HALF):
        mixed = turned[e * TURN_STRIDE : e * TURN_STRIDE + HALF, :]
        square = turned[e * TURN_STRIDE + HALF : e * TURN_STRIDE + TILE, :]
        mixed_t = turned[pl.ds(e, HALF, stride=TURN_STRIDE), :]
        square_t = turned[pl.ds(HALF + e, HALF, stride=TURN_STRIDE), :]
        start = TURN_STRIDE * HALF + (e % 2) * TILE + e
        diagonal = turned[start : start + 1, :]
        first = jnp.where(place >= e, mixed, mixed_t)
        last = jnp.where(place == e, diagonal, jnp.where(place < e, mixed, mixed_t))
        up = jnp.concatenate([first, square], axis=0)
        low = jnp.concatenate([square_t, last], axis=0)
        weights[e * TILE : (e + 1) * TILE, :] = up.astype(BF16)
        weights[(HALF + e) * TILE : (HALF + e + 1) * TILE, :] = low.astype(BF16)
    left = jnp.concatenate([own_ref[0], rest_ref[0]], axis=0)
    acc = jnp.dot(left, weights[...], preferred_element_type=F32)
    for s in range(sources // 8):
        for r in range(targets):
            start = (s * targets + r) * 8
            out_ref[r, s * 8 : (s + 1) * 8, :] = acc[start : start + 8, :]


def contract(packed, own, rest, targets):
    count, groups, small, _ = packed.shape
    _, own_rows, width = own.shape
    rest_rows = rest.shape[1]
    total = own_rows + rest_rows
    return pl.pallas_call(
        contract_kernel,
        out_shape=jax.ShapeDtypeStruct((targets, total // targets, groups * LANES), F32),
        grid_spec=pltpu.PrefetchScalarGridSpec(
            num_scalar_prefetch=0,
            grid=(groups,),
            in_specs=[
                pl.BlockSpec((count, 1, small, PACKED), lambda g: (0, g, 0, 0)),
                pl.BlockSpec((1, own_rows, width), lambda g: (g, 0, 0)),
                pl.BlockSpec((1, rest_rows, width), lambda g: (g, 0, 0)),
            ],
            out_specs=pl.BlockSpec((targets, total // targets, LANES), lambda g: (0, 0, g)),
            scratch_shapes=[
                pltpu.VMEM((TURN_STRIDE * HALF + LANES, LANES), F32),
                pltpu.VMEM((width, LANES), BF16),
            ],
        ),
        compiler_params=pltpu.CompilerParams(vmem_limit_bytes=59 << 20),
        cost_estimate=pl.CostEstimate(flops=6 * 10**9, transcendentals=0, bytes_accessed=2 * 10**7),
        name="contract",
    )(packed, own, rest)


def place_kernel(perm_ref, parts_ref, out_ref, left):
    step = pl.program_id(0)
    sources, rows, width = parts_ref.shape
    total = sources * 8

    @pl.when(step == 0)
    def prepare():
        for y_s in range(SPLIT):
            for z in range(sources // SPLIT):
                for y in range(SPLIT):
                    d = (y_s - y) % SPLIT
                    value = parts_ref[y_s * (sources // SPLIT) + z, d * 8 : (d + 1) * 8, :]
                    start = (y * (sources // SPLIT) + z) * 8
                    left[start : start + 8, y_s * width : (y_s + 1) * width] = value

    value = left[...]
    high = value.astype(BF16)
    value = value - high.astype(F32)
    middle = value.astype(BF16)
    low = (value - middle.astype(F32)).astype(BF16)
    pieces = jnp.concatenate([high, middle, low], axis=0)
    target = lax.broadcasted_iota(jnp.int32, (STEP, perm_ref.shape[1]), 0) + step * STEP
    chosen = jnp.where(perm_ref[...] == target, 1.0, 0.0).astype(BF16)
    out = lax.dot_general(pieces, chosen, (((1,), (1,)), ((), ())), preferred_element_type=F32)
    out = out[:total] + out[total : 2 * total] + out[2 * total :]
    for c in range(STEP // LANES):
        out_ref[c] = out[:, c * LANES : (c + 1) * LANES]


def place(perm, parts):
    sources, rows, width = parts.shape
    columns = perm.shape[1]
    total = sources * 8
    return pl.pallas_call(
        place_kernel,
        out_shape=jax.ShapeDtypeStruct((columns // LANES, total, LANES), F32),
        grid_spec=pltpu.PrefetchScalarGridSpec(
            num_scalar_prefetch=0,
            grid=(columns // STEP,),
            in_specs=[
                pl.BlockSpec((1, columns), lambda g: (0, 0)),
                pl.BlockSpec((sources, rows, width), lambda g: (0, 0, 0)),
            ],
            out_specs=pl.BlockSpec((STEP // LANES, total, LANES), lambda g: (g, 0, 0)),
            scratch_shapes=[pltpu.VMEM((total, columns), F32)],
        ),
        compiler_params=pltpu.CompilerParams(vmem_limit_bytes=40 << 20),
        cost_estimate=pl.CostEstimate(flops=2 * 10**9, transcendentals=0, bytes_accessed=10**6),
        name="place",
    )(perm, parts)


def body(row_size, primal, dual_inv, col_values, col_perm, slab_values, slab_tile):
    count = slab_values.shape[1]
    shared = row_size // SPLIT
    block = lax.axis_index("col")
    y = (lax.axis_index("row").astype(jnp.int32) // shared).reshape(1)

    packed = pack(y, col_values)
    packed = lax.all_to_all(packed, "col", split_axis=0, concat_axis=0, tiled=True)

    message = pack_slab(slab_values, slab_tile)
    arrived = []
    for d in range(1, SPLIT):
        pairs = [(i, (i + d * shared) % row_size) for i in range(row_size)]
        arrived.append(lax.ppermute(message, "row", pairs))

    own, *matrices = make_terms(y, [primal, dual_inv], False, message)
    (rest,) = make_terms(y, matrices, True, *arrived)
    parts = contract(packed, own, rest, row_size)
    parts = lax.all_to_all(parts, "row", split_axis=0, concat_axis=0, tiled=True)
    perm = lax.dynamic_slice_in_dim(col_perm, block, 1, axis=0)
    placed = place(perm, parts)
    placed = lax.all_to_all(placed, "col", split_axis=0, concat_axis=0, tiled=True)
    return jnp.sum(placed, axis=0)


def solution(mesh):
    return jax.shard_map(
        functools.partial(body, mesh.shape["row"]),
        mesh=mesh,
        in_specs=(
            P("col", None, None),
            P("col", None, None),
            P(None, None, "col", None),
            P(),
            P("col", "row", None),
            P("col", "row"),
        ),
        out_specs=P("row", "col"),
        check_vma=False,
    )
```

```python
import functools

import jax
import jax.numpy as jnp
from jax import lax
from jax.experimental import pallas as pl
from jax.experimental.pallas import tpu as pltpu
from jax.sharding import PartitionSpec as P

TILE = 64
HALF = TILE // 2
LANES = 128
PACKED = TILE * HALF + LANES
SPLIT = 4
F32 = jnp.float32
BF16 = jnp.bfloat16


def lane_parts(shape, first_vreg):
    lane = lax.broadcasted_iota(jnp.int32, shape, len(shape) - 1)
    e = lane // TILE + 2 * first_vreg
    h = (lane % TILE) // HALF
    f = lane % HALF
    return e, h, f


def pack_kernel(y_ref, values_ref, out_ref):
    blocks, groups, rows, width = values_ref.shape
    half = width // 2
    count = blocks * groups * rows
    for j in range(half // LANES):
        lanes = slice(j * LANES, (j + 1) * LANES)
        e, h, f = lane_parts((count, LANES), j)
        upper = values_ref[:, :, :, lanes].astype(F32).reshape(count, LANES)
        lower = values_ref[:, :, :, half + j * LANES : half + (j + 1) * LANES].astype(F32).reshape(count, LANES)
        lower = pltpu.roll(lower, LANES - HALF, 1)
        kept = jnp.where((h == 1) | (e <= f), upper, lower)
        extra = jnp.where((h == 0) & (e == f), lower, 0.0 if j == 0 else extra)
        out_ref[:, :, :, lanes] = kept.reshape(blocks, groups, rows, LANES).astype(BF16)
    out_ref[:, :, :, half:] = extra.reshape(blocks, groups, rows, LANES).astype(BF16)


def pack(y, values):
    blocks, tiles, rows, width = values.shape
    groups = tiles // SPLIT
    step = blocks // 2
    return pl.pallas_call(
        pack_kernel,
        out_shape=jax.ShapeDtypeStruct((blocks, groups, rows, PACKED), BF16),
        grid_spec=pltpu.PrefetchScalarGridSpec(
            num_scalar_prefetch=1,
            grid=(blocks // step,),
            in_specs=[pl.BlockSpec((step, groups, rows, width), lambda g, y: (g, y[0], 0, 0))],
            out_specs=pl.BlockSpec((step, groups, rows, PACKED), lambda g, y: (g, 0, 0, 0)),
        ),
        compiler_params=pltpu.CompilerParams(vmem_limit_bytes=59 << 20),
        cost_estimate=pl.CostEstimate(flops=10**7, transcendentals=0, bytes_accessed=7 * 10**6),
        name="pack",
    )(y, values)


def pack_slab_kernel(slab_ref, tile_ref, out_ref):
    half = slab_ref.shape[2] // 2
    count = slab_ref.shape[1]
    extra = jnp.zeros((count, LANES), F32)
    for j in range(half // LANES):
        e, h, f = lane_parts((count, LANES), j)
        upper = slab_ref[0, :, j * LANES : (j + 1) * LANES].astype(F32)
        lower = slab_ref[0, :, half + j * LANES : half + (j + 1) * LANES].astype(F32)
        lower = pltpu.roll(lower, LANES - HALF, 1)
        kept = jnp.where((h == 1) | (e <= f), upper, lower)
        extra = jnp.where((h == 0) & (e == f), lower, extra)
        out_ref[:, j * LANES : (j + 1) * LANES] = kept.astype(BF16)
    ids = tile_ref[...].astype(F32)
    ids = jnp.concatenate([jnp.zeros((1, LANES - count), F32), ids], axis=1)
    lane = lax.broadcasted_iota(jnp.int32, (count, LANES), 1)
    extra = extra + jnp.where(lane < TILE, pltpu.roll(extra, TILE, 1), 0.0)
    out_ref[:, half:] = jnp.where(lane < TILE, extra, ids).astype(BF16)


def pack_slab(slab, tile_of):
    _, count, width = slab.shape
    return pl.pallas_call(
        pack_slab_kernel,
        out_shape=jax.ShapeDtypeStruct((count, PACKED), BF16),
        cost_estimate=pl.CostEstimate(flops=10**6, transcendentals=0, bytes_accessed=10**6),
        name="pack_slab",
    )(slab, tile_of)


def split2(x):
    high = x.astype(BF16)
    low = (x - high.astype(F32)).astype(BF16)
    return high, low


ROWS = 16
EXTRA = 16
OUT_STRIDE = 24
ROW_STRIDE = 40
TURN_STRIDE = 72


def terms_kernel(parts, ready, y_ref, first_ref, second_ref, *refs):
    slabs, tile_rows, refs = refs[:parts], refs[parts : 2 * parts], refs[2 * parts :]
    if ready:
        dual_w, primal_w = first_ref, second_ref
        out_ref, weights, terms, diagonals, tile_rows_i, tile_ids = refs
    else:
        primal_ref, dual_ref = first_ref, second_ref
        out_ref, dual_w, primal_w, weights, terms, diagonals, tile_rows_i, tile_ids, stage = refs
    tiles = dual_w.shape[0]
    groups = out_ref.shape[0]
    step = pl.program_id(0)
    steps = pl.num_programs(0) // len(slabs)
    lane_i = lax.broadcasted_iota(jnp.int32, (HALF, LANES), 1)
    row_i = lax.broadcasted_iota(jnp.int32, (HALF, LANES), 0)
    lane_i2 = lax.broadcasted_iota(jnp.int32, (TILE, LANES), 1)
    low_lanes = lane_i < TILE

    @pl.when(step == 0)
    def prepare():
        for k in range(parts):
            tile_rows_i[k] = tile_rows[k][...].astype(F32).astype(jnp.int32)[:8]
        pltpu.sync_copy(tile_rows_i, tile_ids)
        if ready:
            return
        for t in range(tiles):
            high, low = split2(dual_ref[0, t * TILE : (t + 1) * TILE, :])
            dual_w[t, :TILE, :] = high
            dual_w[t, TILE:, :] = low
        source = lax.broadcasted_iota(jnp.int32, (LANES, 2 * LANES), 0)
        target = lax.broadcasted_iota(jnp.int32, (LANES, 2 * LANES), 1)
        wanted = (target // LANES) * TILE + target % TILE
        spread = jnp.where(source == wanted, 1.0, 0.0).astype(BF16)
        for j in range(tiles // 2):
            stage[...] = primal_ref[0, :, j * LANES : (j + 1) * LANES]
            x = jnp.concatenate(
                [
                    stage[pl.ds(u * TILE + par, HALF, stride=2), :]
                    for u in range(groups)
                    for par in range(2)
                ],
                axis=0,
            )
            for place, part in enumerate(split2(x)):
                part = jnp.dot(part, spread, preferred_element_type=F32).astype(BF16)
                lanes = slice(place * LANES, (place + 1) * LANES)
                primal_w[2 * j, :, lanes] = part[:, :LANES]
                primal_w[2 * j + 1, :, lanes] = part[:, LANES:]

    for k, slab_ref in enumerate(slabs):

        @pl.when(step // steps == k)
        def spread_rows():
            for m in range(HALF // 2):
                part = slab_ref[:, m * LANES : (m + 1) * LANES].astype(F32)
                terms[0, pl.ds(2 * m, ROWS, stride=ROW_STRIDE), :] = part
                terms[0, pl.ds(2 * m + 1, ROWS, stride=ROW_STRIDE), :] = pltpu.roll(part, TILE, 1)
            diagonals[...] = slab_ref[:, TILE * HALF :].astype(F32)

    tile_of = [tile_ids[step // steps, 0, TILE + (step % steps) * ROWS + i] for i in range(ROWS)]

    for i in range(ROWS):
        z = terms[0, i * ROW_STRIDE : i * ROW_STRIDE + HALF, :]
        turned = z.T
        z_t = jnp.concatenate([turned[:HALF], jnp.zeros((HALF, LANES - HALF), F32)], axis=1)
        square_t = jnp.concatenate([turned[HALF:TILE], jnp.zeros((HALF, LANES - HALF), F32)], axis=1)
        top = jnp.where(lane_i >= row_i, z, z_t)
        corner = jnp.where(lane_i < row_i, z, z_t)
        corner = jnp.where(lane_i == row_i, diagonals[i : i + 1, :], corner)
        bottom = jnp.where(lane_i < HALF, square_t, pltpu.roll(corner, HALF, 1))
        square = jnp.concatenate([top, bottom], axis=0)
        square = jnp.where(lane_i2 < TILE, square, pltpu.roll(square, TILE, 1)).astype(BF16)
        panel = jnp.dot(square, dual_w[tile_of[i]], preferred_element_type=F32)
        high, low = split2(panel)
        weights[i, :TILE, :] = high
        weights[i, TILE:, :] = low

    for i in range(ROWS):
        t = tile_of[i]
        right = weights[i]
        product = jnp.dot(primal_w[t], jnp.concatenate([right, right], axis=0), preferred_element_type=F32)
        for pair in range(groups // 2):
            lanes = slice(pair * LANES, (pair + 1) * LANES)
            out = product[pair * LANES : (pair + 1) * LANES, lanes]
            even0, odd0, even1, odd1 = (out[q * HALF : (q + 1) * HALF] for q in range(4))
            mixed = pltpu.roll(jnp.where(low_lanes, odd0, even1), TILE, 1)
            terms[2 * pair, pl.ds(i, HALF, stride=OUT_STRIDE), :] = jnp.where(low_lanes, even0, mixed)
            terms[2 * pair + 1, pl.ds(i, HALF, stride=OUT_STRIDE), :] = jnp.where(low_lanes, mixed, odd1)

    for u in range(groups):
        for m in range(HALF):
            out_ref[u, :, m * LANES : (m + 1) * LANES] = terms[u, m * OUT_STRIDE : m * OUT_STRIDE + ROWS, :].astype(BF16)


def make_terms(y, matrices, ready, *slabs):
    order = matrices[0].shape[1]
    if ready:
        tiles, _, width = matrices[0].shape
    else:
        tiles = order // TILE
        width = order // SPLIT
    groups = width // TILE
    count = slabs[0].shape[0]
    steps = count // ROWS
    total = count * len(slabs)
    ready_shapes = [(tiles, 2 * TILE, width), (tiles, width, 4 * TILE)]

    def whole(shape):
        return pl.BlockSpec(shape, lambda g, y: (0, 0, 0), pipeline_mode=pl.Buffered(1))

    def slab_spec(k):
        return pl.BlockSpec(
            (ROWS, PACKED),
            lambda g, y: (jnp.clip(g - k * steps, 0, steps - 1), 0),
        )

    if ready:
        matrix_specs = [whole(shape) for shape in ready_shapes]
    else:
        matrix_specs = [
            pl.BlockSpec((1, width, order), lambda g, y: (0, y[0], 0)),
            pl.BlockSpec((1, order, width), lambda g, y: (0, 0, y[0])),
        ]
    out_shape = [jax.ShapeDtypeStruct((groups, total, TILE * TILE), BF16)]
    out_specs = [pl.BlockSpec((groups, ROWS, TILE * TILE), lambda g, y: (0, g, 0))]
    scratch = [
        pltpu.VMEM((ROWS, 2 * TILE, width), BF16),
        pltpu.VMEM((groups, HALF * OUT_STRIDE, LANES), F32),
        pltpu.VMEM((ROWS, LANES), F32),
        pltpu.VMEM((len(slabs), 8, LANES), jnp.int32),
        pltpu.SMEM((len(slabs), 8, LANES), jnp.int32),
    ]
    if not ready:
        out_shape += [jax.ShapeDtypeStruct(shape, BF16) for shape in ready_shapes]
        out_specs += [whole(shape) for shape in ready_shapes]
        scratch += [pltpu.VMEM((width, LANES), F32)]
    return pl.pallas_call(
        functools.partial(terms_kernel, len(slabs), ready),
        out_shape=out_shape,
        grid_spec=pltpu.PrefetchScalarGridSpec(
            num_scalar_prefetch=1,
            grid=(total // ROWS,),
            in_specs=[
                *matrix_specs,
                *(slab_spec(k) for k in range(len(slabs))),
                *(
                    pl.BlockSpec((EXTRA, LANES), lambda g, y: (0, TILE * HALF // LANES))
                    for _ in slabs
                ),
            ],
            out_specs=out_specs,
            scratch_shapes=scratch,
        ),
        compiler_params=pltpu.CompilerParams(vmem_limit_bytes=58 << 20),
        cost_estimate=pl.CostEstimate(
            flops=total * 10**8, transcendentals=0, bytes_accessed=2 * 10**6 + total * 40000
        ),
        name="terms",
    )(y, *matrices, *slabs, *slabs)


STEP = 256


def contract_kernel(packed_ref, own_ref, rest_ref, out_ref, turned, weights):
    group = pl.program_id(0)
    count, _, small, _ = packed_ref.shape
    targets, sources, _ = out_ref.shape
    for v in range(PACKED // LANES):
        lanes = slice(v * LANES, (v + 1) * LANES)
        part = packed_ref[:, 0, :, lanes].astype(F32).reshape(count * small, LANES)
        part = part.T
        if v < HALF // 2:
            for k in range(2):
                turned[(2 * v + k) * TURN_STRIDE : (2 * v + k) * TURN_STRIDE + TILE, :] = part[k * TILE : (k + 1) * TILE]
        else:
            turned[HALF * TURN_STRIDE :, :] = part
    place = lax.broadcasted_iota(jnp.int32, (HALF, LANES), 0)
    for e in range(HALF):
        mixed = turned[e * TURN_STRIDE : e * TURN_STRIDE + HALF, :]
        square = turned[e * TURN_STRIDE + HALF : e * TURN_STRIDE + TILE, :]
        mixed_t = turned[pl.ds(e, HALF, stride=TURN_STRIDE), :]
        square_t = turned[pl.ds(HALF + e, HALF, stride=TURN_STRIDE), :]
        start = TURN_STRIDE * HALF + (e % 2) * TILE + e
        diagonal = turned[start : start + 1, :]
        first = jnp.where(place >= e, mixed, mixed_t)
        last = jnp.where(place == e, diagonal, jnp.where(place < e, mixed, mixed_t))
        up = jnp.concatenate([first, square], axis=0)
        low = jnp.concatenate([square_t, last], axis=0)
        weights[e * TILE : (e + 1) * TILE, :] = up.astype(BF16)
        weights[(HALF + e) * TILE : (HALF + e + 1) * TILE, :] = low.astype(BF16)
    left = jnp.concatenate([own_ref[0], rest_ref[0]], axis=0)
    acc = jnp.dot(left, weights[...], preferred_element_type=F32)
    for r in range(targets):
        starts = [(s * targets + r) * 8 for s in range(sources // 8)]
        mine = jnp.concatenate([acc[start : start + 8, :] for start in starts], axis=0)
        out_ref[r] = mine.astype(BF16)


def contract(packed, own, rest, targets):
    count, groups, small, _ = packed.shape
    _, own_rows, width = own.shape
    rest_rows = rest.shape[1]
    total = own_rows + rest_rows
    return pl.pallas_call(
        contract_kernel,
        out_shape=jax.ShapeDtypeStruct((targets, total // targets, groups * LANES), BF16),
        grid_spec=pltpu.PrefetchScalarGridSpec(
            num_scalar_prefetch=0,
            grid=(groups,),
            in_specs=[
                pl.BlockSpec((count, 1, small, PACKED), lambda g: (0, g, 0, 0)),
                pl.BlockSpec((1, own_rows, width), lambda g: (g, 0, 0)),
                pl.BlockSpec((1, rest_rows, width), lambda g: (g, 0, 0)),
            ],
            out_specs=pl.BlockSpec((targets, total // targets, LANES), lambda g: (0, 0, g)),
            scratch_shapes=[
                pltpu.VMEM((TURN_STRIDE * HALF + LANES, LANES), F32),
                pltpu.VMEM((width, LANES), BF16),
            ],
        ),
        compiler_params=pltpu.CompilerParams(vmem_limit_bytes=50 << 20),
        cost_estimate=pl.CostEstimate(flops=6 * 10**9, transcendentals=0, bytes_accessed=2 * 10**7),
        name="contract",
    )(packed, own, rest)


def place_kernel(perm_ref, parts_ref, out_ref, left):
    step = pl.program_id(0)
    sources, rows, width = parts_ref.shape
    total = sources * 8

    @pl.when(step == 0)
    def prepare():
        shared = sources // SPLIT
        for y_s in range(SPLIT):
            arrived = [parts_ref[y_s * shared + z].astype(F32) for z in range(shared)]
            rows = []
            for y in range(SPLIT):
                d = (y_s - y) % SPLIT
                rows += [arrived[z][d * 8 : (d + 1) * 8] for z in range(shared)]
            left[:, y_s * width : (y_s + 1) * width] = jnp.concatenate(rows, axis=0).astype(BF16)

    target = lax.broadcasted_iota(jnp.int32, (STEP, perm_ref.shape[1]), 0) + step * STEP
    chosen = jnp.where(perm_ref[...] == target, 1.0, 0.0).astype(BF16)
    out = lax.dot_general(left[...], chosen, (((1,), (1,)), ((), ())), preferred_element_type=F32)
    for c in range(STEP // LANES):
        out_ref[c] = out[:, c * LANES : (c + 1) * LANES].astype(BF16)


def place(perm, parts):
    sources, rows, width = parts.shape
    columns = perm.shape[1]
    total = sources * 8
    return pl.pallas_call(
        place_kernel,
        out_shape=jax.ShapeDtypeStruct((columns // LANES, total, LANES), BF16),
        grid_spec=pltpu.PrefetchScalarGridSpec(
            num_scalar_prefetch=0,
            grid=(columns // STEP,),
            in_specs=[
                pl.BlockSpec((1, columns), lambda g: (0, 0)),
                pl.BlockSpec((sources, rows, width), lambda g: (0, 0, 0)),
            ],
            out_specs=pl.BlockSpec((STEP // LANES, total, LANES), lambda g: (g, 0, 0)),
            scratch_shapes=[pltpu.VMEM((total, columns), BF16)],
        ),
        compiler_params=pltpu.CompilerParams(vmem_limit_bytes=40 << 20),
        cost_estimate=pl.CostEstimate(flops=2 * 10**9, transcendentals=0, bytes_accessed=10**6),
        name="place",
    )(perm, parts)


def body(row_size, primal, dual_inv, col_values, col_perm, slab_values, slab_tile):
    count = slab_values.shape[1]
    shared = row_size // SPLIT
    block = lax.axis_index("col")
    y = (lax.axis_index("row").astype(jnp.int32) // shared).reshape(1)

    packed = pack(y, col_values)
    packed = lax.all_to_all(packed, "col", split_axis=0, concat_axis=0, tiled=True)

    message = pack_slab(slab_values, slab_tile)
    arrived = []
    for d in range(1, SPLIT):
        pairs = [(i, (i + d * shared) % row_size) for i in range(row_size)]
        arrived.append(lax.ppermute(message, "row", pairs))

    own, *matrices = make_terms(y, [primal, dual_inv], False, message)
    (rest,) = make_terms(y, matrices, True, *arrived)
    parts = contract(packed, own, rest, row_size)
    parts = lax.all_to_all(parts, "row", split_axis=0, concat_axis=0, tiled=True)
    perm = lax.dynamic_slice_in_dim(col_perm, block, 1, axis=0)
    placed = place(perm, parts)
    placed = lax.all_to_all(placed, "col", split_axis=0, concat_axis=0, tiled=True)
    return jnp.sum(placed.astype(F32), axis=0)


def solution(mesh):
    return jax.shard_map(
        functools.partial(body, mesh.shape["row"]),
        mesh=mesh,
        in_specs=(
            P("col", None, None),
            P("col", None, None),
            P(None, None, "col", None),
            P(),
            P("col", "row", None),
            P("col", "row"),
        ),
        out_specs=P("row", "col"),
        check_vma=False,
    )
```

```python
import functools

import jax
import jax.numpy as jnp
from jax import lax
from jax.experimental import pallas as pl
from jax.experimental.pallas import tpu as pltpu
from jax.sharding import PartitionSpec as P

TILE = 64
HALF = TILE // 2
LANES = 128
PACKED = TILE * HALF + LANES
SPLIT = 4
F32 = jnp.float32
BF16 = jnp.bfloat16


def lane_parts(shape, first_vreg):
    lane = lax.broadcasted_iota(jnp.int32, shape, len(shape) - 1)
    e = lane // TILE + 2 * first_vreg
    h = (lane % TILE) // HALF
    f = lane % HALF
    return e, h, f


def pack_kernel(y_ref, values_ref, out_ref):
    blocks, groups, rows, width = values_ref.shape
    half = width // 2
    count = blocks * groups * rows
    for j in range(half // LANES):
        lanes = slice(j * LANES, (j + 1) * LANES)
        e, h, f = lane_parts((count, LANES), j)
        upper = values_ref[:, :, :, lanes].astype(F32).reshape(count, LANES)
        lower = values_ref[:, :, :, half + j * LANES : half + (j + 1) * LANES].astype(F32).reshape(count, LANES)
        lower = pltpu.roll(lower, LANES - HALF, 1)
        kept = jnp.where((h == 1) | (e <= f), upper, lower)
        extra = jnp.where((h == 0) & (e == f), lower, 0.0 if j == 0 else extra)
        out_ref[:, :, :, lanes] = kept.reshape(blocks, groups, rows, LANES).astype(BF16)
    out_ref[:, :, :, half:] = extra.reshape(blocks, groups, rows, LANES).astype(BF16)


def pack(y, values):
    blocks, tiles, rows, width = values.shape
    groups = tiles // SPLIT
    step = blocks // 2
    return pl.pallas_call(
        pack_kernel,
        out_shape=jax.ShapeDtypeStruct((blocks, groups, rows, PACKED), BF16),
        grid_spec=pltpu.PrefetchScalarGridSpec(
            num_scalar_prefetch=1,
            grid=(blocks // step,),
            in_specs=[pl.BlockSpec((step, groups, rows, width), lambda g, y: (g, y[0], 0, 0))],
            out_specs=pl.BlockSpec((step, groups, rows, PACKED), lambda g, y: (g, 0, 0, 0)),
        ),
        compiler_params=pltpu.CompilerParams(vmem_limit_bytes=59 << 20),
        cost_estimate=pl.CostEstimate(flops=10**7, transcendentals=0, bytes_accessed=7 * 10**6),
        name="pack",
    )(y, values)


def pack_slab_kernel(slab_ref, tile_ref, out_ref):
    half = slab_ref.shape[2] // 2
    count = slab_ref.shape[1]
    extra = jnp.zeros((count, LANES), F32)
    for j in range(half // LANES):
        e, h, f = lane_parts((count, LANES), j)
        upper = slab_ref[0, :, j * LANES : (j + 1) * LANES].astype(F32)
        lower = slab_ref[0, :, half + j * LANES : half + (j + 1) * LANES].astype(F32)
        lower = pltpu.roll(lower, LANES - HALF, 1)
        kept = jnp.where((h == 1) | (e <= f), upper, lower)
        extra = jnp.where((h == 0) & (e == f), lower, extra)
        out_ref[:, j * LANES : (j + 1) * LANES] = kept.astype(BF16)
    ids = tile_ref[...].astype(F32)
    ids = jnp.concatenate([jnp.zeros((1, LANES - count), F32), ids], axis=1)
    lane = lax.broadcasted_iota(jnp.int32, (count, LANES), 1)
    extra = extra + jnp.where(lane < TILE, pltpu.roll(extra, TILE, 1), 0.0)
    out_ref[:, half:] = jnp.where(lane < TILE, extra, ids).astype(BF16)


def pack_slab(slab, tile_of):
    _, count, width = slab.shape
    return pl.pallas_call(
        pack_slab_kernel,
        out_shape=jax.ShapeDtypeStruct((count, PACKED), BF16),
        cost_estimate=pl.CostEstimate(flops=10**6, transcendentals=0, bytes_accessed=10**6),
        name="pack_slab",
    )(slab, tile_of)


def split2(x):
    high = x.astype(BF16)
    low = (x - high.astype(F32)).astype(BF16)
    return high, low


ROWS = 64
EXTRA = 16
OUT_STRIDE = 72
ROW_STRIDE = 40
TURN_STRIDE = 72


def terms_kernel(parts, y_ref, primal_ref, dual_ref, *refs):
    slabs, tile_rows, refs = refs[:parts], refs[parts : 2 * parts], refs[2 * parts :]
    out_ref, weights, terms, diagonals, tile_rows_i, tile_ids, stage, dual_w, primal_w = refs
    tiles = dual_w.shape[0]
    groups = out_ref.shape[0]
    step = pl.program_id(0)
    steps = pl.num_programs(0) // len(slabs)
    lane_i = lax.broadcasted_iota(jnp.int32, (HALF, LANES), 1)
    row_i = lax.broadcasted_iota(jnp.int32, (HALF, LANES), 0)
    lane_i2 = lax.broadcasted_iota(jnp.int32, (TILE, LANES), 1)
    low_lanes = lane_i < TILE

    @pl.when(step == 0)
    def prepare():
        for k in range(parts):
            tile_rows_i[k] = tile_rows[k][...].astype(F32).astype(jnp.int32)[:8]
        pltpu.sync_copy(tile_rows_i, tile_ids)
        for t in range(tiles):
            high, low = split2(dual_ref[0, t * TILE : (t + 1) * TILE, :])
            dual_w[t, :TILE, :] = high
            dual_w[t, TILE:, :] = low
        source = lax.broadcasted_iota(jnp.int32, (LANES, 2 * LANES), 0)
        target = lax.broadcasted_iota(jnp.int32, (LANES, 2 * LANES), 1)
        wanted = (target // LANES) * TILE + target % TILE
        spread = jnp.where(source == wanted, 1.0, 0.0).astype(BF16)
        for j in range(tiles // 2):
            stage[...] = primal_ref[0, :, j * LANES : (j + 1) * LANES]
            x = jnp.concatenate(
                [
                    stage[pl.ds(u * TILE + par, HALF, stride=2), :]
                    for u in range(groups)
                    for par in range(2)
                ],
                axis=0,
            )
            for place, part in enumerate(split2(x)):
                part = jnp.dot(part, spread, preferred_element_type=F32).astype(BF16)
                lanes = slice(place * LANES, (place + 1) * LANES)
                primal_w[2 * j, :, lanes] = part[:, :LANES]
                primal_w[2 * j + 1, :, lanes] = part[:, LANES:]

    for k, slab_ref in enumerate(slabs):

        @pl.when(step // steps == k)
        def spread_rows():
            for m in range(HALF // 2):
                part = slab_ref[:, m * LANES : (m + 1) * LANES].astype(F32)
                terms[0, pl.ds(2 * m, ROWS, stride=ROW_STRIDE), :] = part
                terms[0, pl.ds(2 * m + 1, ROWS, stride=ROW_STRIDE), :] = pltpu.roll(part, TILE, 1)
            diagonals[...] = slab_ref[:, TILE * HALF :].astype(F32)

    tile_of = [tile_ids[step // steps, 0, TILE + (step % steps) * ROWS + i] for i in range(ROWS)]

    for i in range(ROWS):
        z = terms[0, i * ROW_STRIDE : i * ROW_STRIDE + HALF, :]
        turned = z.T
        z_t = jnp.concatenate([turned[:HALF], jnp.zeros((HALF, LANES - HALF), F32)], axis=1)
        square_t = jnp.concatenate([turned[HALF:TILE], jnp.zeros((HALF, LANES - HALF), F32)], axis=1)
        top = jnp.where(lane_i >= row_i, z, z_t)
        corner = jnp.where(lane_i < row_i, z, z_t)
        corner = jnp.where(lane_i == row_i, diagonals[i : i + 1, :], corner)
        bottom = jnp.where(lane_i < HALF, square_t, pltpu.roll(corner, HALF, 1))
        square = jnp.concatenate([top, bottom], axis=0)
        square = jnp.where(lane_i2 < TILE, square, pltpu.roll(square, TILE, 1)).astype(BF16)
        panel = jnp.dot(square, dual_w[tile_of[i]], preferred_element_type=F32)
        high, low = split2(panel)
        weights[i, :TILE, :] = high
        weights[i, TILE:, :] = low

    for i in range(ROWS):
        t = tile_of[i]
        right = weights[i]
        product = jnp.dot(primal_w[t], jnp.concatenate([right, right], axis=0), preferred_element_type=F32)
        for pair in range(groups // 2):
            lanes = slice(pair * LANES, (pair + 1) * LANES)
            out = product[pair * LANES : (pair + 1) * LANES, lanes]
            even0, odd0, even1, odd1 = (out[q * HALF : (q + 1) * HALF] for q in range(4))
            mixed = pltpu.roll(jnp.where(low_lanes, odd0, even1), TILE, 1)
            terms[2 * pair, pl.ds(i, HALF, stride=OUT_STRIDE), :] = jnp.where(low_lanes, even0, mixed)
            terms[2 * pair + 1, pl.ds(i, HALF, stride=OUT_STRIDE), :] = jnp.where(low_lanes, mixed, odd1)

    for u in range(groups):
        for m in range(HALF):
            out_ref[u, :, m * LANES : (m + 1) * LANES] = terms[u, m * OUT_STRIDE : m * OUT_STRIDE + ROWS, :].astype(BF16)


def make_terms(y, primal, dual, *slabs):
    order = primal.shape[1]
    tiles = order // TILE
    width = order // SPLIT
    groups = width // TILE
    count = slabs[0].shape[0]
    steps = count // ROWS
    total = count * len(slabs)

    def slab_spec(k):
        return pl.BlockSpec(
            (ROWS, PACKED),
            lambda g, y: (jnp.clip(g - k * steps, 0, steps - 1), 0),
        )

    scratch = [
        pltpu.VMEM((ROWS, 2 * TILE, width), BF16),
        pltpu.VMEM((groups, max(HALF * OUT_STRIDE, ROWS * ROW_STRIDE), LANES), F32),
        pltpu.VMEM((ROWS, LANES), F32),
        pltpu.VMEM((len(slabs), 8, LANES), jnp.int32),
        pltpu.SMEM((len(slabs), 8, LANES), jnp.int32),
        pltpu.VMEM((width, LANES), F32),
        pltpu.VMEM((tiles, 2 * TILE, width), BF16),
        pltpu.VMEM((tiles, width, 4 * TILE), BF16),
    ]
    return pl.pallas_call(
        functools.partial(terms_kernel, len(slabs)),
        out_shape=jax.ShapeDtypeStruct((groups, total, TILE * TILE), BF16),
        grid_spec=pltpu.PrefetchScalarGridSpec(
            num_scalar_prefetch=1,
            grid=(total // ROWS,),
            in_specs=[
                pl.BlockSpec((1, width, order), lambda g, y: (0, y[0], 0)),
                pl.BlockSpec((1, order, width), lambda g, y: (0, 0, y[0])),
                *(slab_spec(k) for k in range(len(slabs))),
                *(
                    pl.BlockSpec((EXTRA, LANES), lambda g, y: (0, TILE * HALF // LANES))
                    for _ in slabs
                ),
            ],
            out_specs=pl.BlockSpec((groups, ROWS, TILE * TILE), lambda g, y: (0, g, 0)),
            scratch_shapes=scratch,
        ),
        compiler_params=pltpu.CompilerParams(vmem_limit_bytes=58 << 20),
        cost_estimate=pl.CostEstimate(
            flops=total * 10**8, transcendentals=0, bytes_accessed=2 * 10**6 + total * 40000
        ),
        name="terms",
    )(y, primal, dual, *slabs, *slabs)


STEP = 256


def contract_kernel(packed_ref, own_ref, rest_ref, out_ref, turned, weights):
    group = pl.program_id(0)
    count, _, small, _ = packed_ref.shape
    targets, sources, _ = out_ref.shape
    for v in range(PACKED // LANES):
        lanes = slice(v * LANES, (v + 1) * LANES)
        part = packed_ref[:, 0, :, lanes].astype(F32).reshape(count * small, LANES)
        part = part.T
        if v < HALF // 2:
            for k in range(2):
                turned[(2 * v + k) * TURN_STRIDE : (2 * v + k) * TURN_STRIDE + TILE, :] = part[k * TILE : (k + 1) * TILE]
        else:
            turned[HALF * TURN_STRIDE :, :] = part
    place = lax.broadcasted_iota(jnp.int32, (HALF, LANES), 0)
    for e in range(HALF):
        mixed = turned[e * TURN_STRIDE : e * TURN_STRIDE + HALF, :]
        square = turned[e * TURN_STRIDE + HALF : e * TURN_STRIDE + TILE, :]
        mixed_t = turned[pl.ds(e, HALF, stride=TURN_STRIDE), :]
        square_t = turned[pl.ds(HALF + e, HALF, stride=TURN_STRIDE), :]
        start = TURN_STRIDE * HALF + (e % 2) * TILE + e
        diagonal = turned[start : start + 1, :]
        first = jnp.where(place >= e, mixed, mixed_t)
        last = jnp.where(place == e, diagonal, jnp.where(place < e, mixed, mixed_t))
        up = jnp.concatenate([first, square], axis=0)
        low = jnp.concatenate([square_t, last], axis=0)
        weights[e * TILE : (e + 1) * TILE, :] = up.astype(BF16)
        weights[(HALF + e) * TILE : (HALF + e + 1) * TILE, :] = low.astype(BF16)
    left = jnp.concatenate([own_ref[0], rest_ref[0]], axis=0)
    acc = jnp.dot(left, weights[...], preferred_element_type=F32)
    for r in range(targets):
        starts = [(s * targets + r) * 8 for s in range(sources // 8)]
        mine = jnp.concatenate([acc[start : start + 8, :] for start in starts], axis=0)
        out_ref[r] = mine.astype(BF16)


def contract(packed, own, rest, targets):
    count, groups, small, _ = packed.shape
    _, own_rows, width = own.shape
    rest_rows = rest.shape[1]
    total = own_rows + rest_rows
    return pl.pallas_call(
        contract_kernel,
        out_shape=jax.ShapeDtypeStruct((targets, total // targets, groups * LANES), BF16),
        grid_spec=pltpu.PrefetchScalarGridSpec(
            num_scalar_prefetch=0,
            grid=(groups,),
            in_specs=[
                pl.BlockSpec((count, 1, small, PACKED), lambda g: (0, g, 0, 0)),
                pl.BlockSpec((1, own_rows, width), lambda g: (g, 0, 0)),
                pl.BlockSpec((1, rest_rows, width), lambda g: (g, 0, 0)),
            ],
            out_specs=pl.BlockSpec((targets, total // targets, LANES), lambda g: (0, 0, g)),
            scratch_shapes=[
                pltpu.VMEM((TURN_STRIDE * HALF + LANES, LANES), F32),
                pltpu.VMEM((width, LANES), BF16),
            ],
        ),
        compiler_params=pltpu.CompilerParams(vmem_limit_bytes=50 << 20),
        cost_estimate=pl.CostEstimate(flops=6 * 10**9, transcendentals=0, bytes_accessed=2 * 10**7),
        name="contract",
    )(packed, own, rest)


def place_kernel(perm_ref, parts_ref, out_ref, left):
    step = pl.program_id(0)
    sources, rows, width = parts_ref.shape
    total = sources * 8

    @pl.when(step == 0)
    def prepare():
        shared = sources // SPLIT
        for y_s in range(SPLIT):
            arrived = [parts_ref[y_s * shared + z].astype(F32) for z in range(shared)]
            rows = []
            for y in range(SPLIT):
                d = (y_s - y) % SPLIT
                rows += [arrived[z][d * 8 : (d + 1) * 8] for z in range(shared)]
            left[:, y_s * width : (y_s + 1) * width] = jnp.concatenate(rows, axis=0).astype(BF16)

    target = lax.broadcasted_iota(jnp.int32, (STEP, perm_ref.shape[1]), 0) + step * STEP
    chosen = jnp.where(perm_ref[...] == target, 1.0, 0.0).astype(BF16)
    out = lax.dot_general(left[...], chosen, (((1,), (1,)), ((), ())), preferred_element_type=F32)
    for c in range(STEP // LANES):
        out_ref[c] = out[:, c * LANES : (c + 1) * LANES].astype(BF16)


def place(perm, parts):
    sources, rows, width = parts.shape
    columns = perm.shape[1]
    total = sources * 8
    return pl.pallas_call(
        place_kernel,
        out_shape=jax.ShapeDtypeStruct((columns // LANES, total, LANES), BF16),
        grid_spec=pltpu.PrefetchScalarGridSpec(
            num_scalar_prefetch=0,
            grid=(columns // STEP,),
            in_specs=[
                pl.BlockSpec((1, columns), lambda g: (0, 0)),
                pl.BlockSpec((sources, rows, width), lambda g: (0, 0, 0)),
            ],
            out_specs=pl.BlockSpec((STEP // LANES, total, LANES), lambda g: (g, 0, 0)),
            scratch_shapes=[pltpu.VMEM((total, columns), BF16)],
        ),
        compiler_params=pltpu.CompilerParams(vmem_limit_bytes=40 << 20),
        cost_estimate=pl.CostEstimate(flops=2 * 10**9, transcendentals=0, bytes_accessed=10**6),
        name="place",
    )(perm, parts)


def body(row_size, primal, dual_inv, col_values, col_perm, slab_values, slab_tile):
    count = slab_values.shape[1]
    shared = row_size // SPLIT
    block = lax.axis_index("col")
    y = (lax.axis_index("row").astype(jnp.int32) // shared).reshape(1)

    packed = pack(y, col_values)
    packed = lax.all_to_all(packed, "col", split_axis=0, concat_axis=0, tiled=True)

    message = pack_slab(slab_values, slab_tile)
    arrived = []
    for d in range(1, SPLIT):
        pairs = [(i, (i + d * shared) % row_size) for i in range(row_size)]
        arrived.append(lax.ppermute(message, "row", pairs))

    own = make_terms(y, primal, dual_inv, message)
    rest = make_terms(y, primal, dual_inv, *arrived)
    parts = contract(packed, own, rest, row_size)
    parts = lax.all_to_all(parts, "row", split_axis=0, concat_axis=0, tiled=True)
    perm = lax.dynamic_slice_in_dim(col_perm, block, 1, axis=0)
    placed = place(perm, parts)
    placed = lax.all_to_all(placed, "col", split_axis=0, concat_axis=0, tiled=True)
    return jnp.sum(placed.astype(F32), axis=0)


def solution(mesh):
    return jax.shard_map(
        functools.partial(body, mesh.shape["row"]),
        mesh=mesh,
        in_specs=(
            P("col", None, None),
            P("col", None, None),
            P(None, None, "col", None),
            P(),
            P("col", "row", None),
            P("col", "row"),
        ),
        out_specs=P("row", "col"),
        check_vma=False,
    )
```

```python
import functools

import jax
import jax.numpy as jnp
from jax import lax
from jax.experimental import pallas as pl
from jax.experimental.pallas import tpu as pltpu
from jax.sharding import PartitionSpec as P

TILE = 64
HALF = TILE // 2
LANES = 128
PACKED = TILE * HALF + LANES
SPLIT = 4
F32 = jnp.float32
BF16 = jnp.bfloat16


def lane_parts(shape, first_vreg):
    lane = lax.broadcasted_iota(jnp.int32, shape, len(shape) - 1)
    e = lane // TILE + 2 * first_vreg
    h = (lane % TILE) // HALF
    f = lane % HALF
    return e, h, f


def pack_kernel(y_ref, values_ref, out_ref):
    blocks, groups, rows, width = values_ref.shape
    half = width // 2
    count = blocks * groups * rows
    for j in range(half // LANES):
        lanes = slice(j * LANES, (j + 1) * LANES)
        e, h, f = lane_parts((count, LANES), j)
        upper = values_ref[:, :, :, lanes].astype(F32).reshape(count, LANES)
        lower = values_ref[:, :, :, half + j * LANES : half + (j + 1) * LANES].astype(F32).reshape(count, LANES)
        lower = pltpu.roll(lower, LANES - HALF, 1)
        kept = jnp.where((h == 1) | (e <= f), upper, lower)
        extra = jnp.where((h == 0) & (e == f), lower, 0.0 if j == 0 else extra)
        out_ref[:, :, :, lanes] = kept.reshape(blocks, groups, rows, LANES).astype(BF16)
    out_ref[:, :, :, half:] = extra.reshape(blocks, groups, rows, LANES).astype(BF16)


def pack(y, values):
    blocks, tiles, rows, width = values.shape
    groups = tiles // SPLIT
    step = blocks // 2
    return pl.pallas_call(
        pack_kernel,
        out_shape=jax.ShapeDtypeStruct((blocks, groups, rows, PACKED), BF16),
        grid_spec=pltpu.PrefetchScalarGridSpec(
            num_scalar_prefetch=1,
            grid=(blocks // step,),
            in_specs=[pl.BlockSpec((step, groups, rows, width), lambda g, y: (g, y[0], 0, 0))],
            out_specs=pl.BlockSpec((step, groups, rows, PACKED), lambda g, y: (g, 0, 0, 0)),
        ),
        compiler_params=pltpu.CompilerParams(vmem_limit_bytes=59 << 20),
        cost_estimate=pl.CostEstimate(flops=10**7, transcendentals=0, bytes_accessed=7 * 10**6),
        name="pack",
    )(y, values)


def pack_slab_kernel(slab_ref, tile_ref, out_ref):
    half = slab_ref.shape[2] // 2
    count = slab_ref.shape[1]
    extra = jnp.zeros((count, LANES), F32)
    for j in range(half // LANES):
        e, h, f = lane_parts((count, LANES), j)
        upper = slab_ref[0, :, j * LANES : (j + 1) * LANES].astype(F32)
        lower = slab_ref[0, :, half + j * LANES : half + (j + 1) * LANES].astype(F32)
        lower = pltpu.roll(lower, LANES - HALF, 1)
        kept = jnp.where((h == 1) | (e <= f), upper, lower)
        extra = jnp.where((h == 0) & (e == f), lower, extra)
        out_ref[:, j * LANES : (j + 1) * LANES] = kept.astype(BF16)
    ids = tile_ref[...].astype(F32)
    ids = jnp.concatenate([jnp.zeros((1, LANES - count), F32), ids], axis=1)
    lane = lax.broadcasted_iota(jnp.int32, (count, LANES), 1)
    extra = extra + jnp.where(lane < TILE, pltpu.roll(extra, TILE, 1), 0.0)
    out_ref[:, half:] = jnp.where(lane < TILE, extra, ids).astype(BF16)


def pack_slab(slab, tile_of):
    _, count, width = slab.shape
    return pl.pallas_call(
        pack_slab_kernel,
        out_shape=jax.ShapeDtypeStruct((count, PACKED), BF16),
        cost_estimate=pl.CostEstimate(flops=10**6, transcendentals=0, bytes_accessed=10**6),
        name="pack_slab",
    )(slab, tile_of)


def split2(x):
    high = x.astype(BF16)
    low = (x - high.astype(F32)).astype(BF16)
    return high, low


ROWS = 64
EXTRA = 16
OUT_STRIDE = 72
ROW_STRIDE = 40
TURN_STRIDE = 72


def terms_kernel(parts, y_ref, primal_ref, dual_ref, *refs):
    slabs, tile_rows, refs = refs[:parts], refs[parts : 2 * parts], refs[2 * parts :]
    out_ref, weights, terms, diagonals, tile_rows_i, tile_ids, stage, dual_w, primal_w = refs
    tiles = dual_w.shape[0]
    groups = out_ref.shape[0]
    step = pl.program_id(0)
    steps = pl.num_programs(0) // len(slabs)
    lane_i = lax.broadcasted_iota(jnp.int32, (HALF, LANES), 1)
    row_i = lax.broadcasted_iota(jnp.int32, (HALF, LANES), 0)
    lane_i2 = lax.broadcasted_iota(jnp.int32, (TILE, LANES), 1)
    low_lanes = lane_i < TILE

    @pl.when(step == 0)
    def prepare():
        for k in range(parts):
            tile_rows_i[k] = tile_rows[k][...].astype(F32).astype(jnp.int32)[:8]
        pltpu.sync_copy(tile_rows_i, tile_ids)
        for t in range(tiles):
            high, low = split2(dual_ref[0, t * TILE : (t + 1) * TILE, :])
            dual_w[t, :TILE, :] = high
            dual_w[t, TILE:, :] = low
        source = lax.broadcasted_iota(jnp.int32, (LANES, 2 * LANES), 0)
        target = lax.broadcasted_iota(jnp.int32, (LANES, 2 * LANES), 1)
        wanted = (target // LANES) * TILE + target % TILE
        spread = jnp.where(source == wanted, 1.0, 0.0).astype(BF16)
        for j in range(tiles // 2):
            stage[...] = primal_ref[0, :, j * LANES : (j + 1) * LANES]
            x = jnp.concatenate(
                [
                    stage[pl.ds(u * TILE + par, HALF, stride=2), :]
                    for u in range(groups)
                    for par in range(2)
                ],
                axis=0,
            )
            for place, part in enumerate(split2(x)):
                part = jnp.dot(part, spread, preferred_element_type=F32).astype(BF16)
                lanes = slice(place * LANES, (place + 1) * LANES)
                primal_w[2 * j, :, lanes] = part[:, :LANES]
                primal_w[2 * j + 1, :, lanes] = part[:, LANES:]

    for k, slab_ref in enumerate(slabs):

        @pl.when(step // steps == k)
        def spread_rows():
            for m in range(HALF // 2):
                part = slab_ref[:, m * LANES : (m + 1) * LANES].astype(F32)
                terms[0, pl.ds(2 * m, ROWS, stride=ROW_STRIDE), :] = part
                terms[0, pl.ds(2 * m + 1, ROWS, stride=ROW_STRIDE), :] = pltpu.roll(part, TILE, 1)
            diagonals[...] = slab_ref[:, TILE * HALF :].astype(F32)

    tile_of = [tile_ids[step // steps, 0, TILE + (step % steps) * ROWS + i] for i in range(ROWS)]

    for i in range(ROWS):
        z = terms[0, i * ROW_STRIDE : i * ROW_STRIDE + HALF, :]
        turned = z.T
        z_t = jnp.concatenate([turned[:HALF], jnp.zeros((HALF, LANES - HALF), F32)], axis=1)
        square_t = jnp.concatenate([turned[HALF:TILE], jnp.zeros((HALF, LANES - HALF), F32)], axis=1)
        top = jnp.where(lane_i >= row_i, z, z_t)
        corner = jnp.where(lane_i < row_i, z, z_t)
        corner = jnp.where(lane_i == row_i, diagonals[i : i + 1, :], corner)
        bottom = jnp.where(lane_i < HALF, square_t, pltpu.roll(corner, HALF, 1))
        square = jnp.concatenate([top, bottom], axis=0)
        square = jnp.where(lane_i2 < TILE, square, pltpu.roll(square, TILE, 1)).astype(BF16)
        panel = jnp.dot(square, dual_w[tile_of[i]], preferred_element_type=F32)
        high, low = split2(panel)
        weights[i, :TILE, :] = high
        weights[i, TILE:, :] = low

    for i in range(ROWS):
        t = tile_of[i]
        right = weights[i]
        product = jnp.dot(primal_w[t], jnp.concatenate([right, right], axis=0), preferred_element_type=F32)
        for pair in range(groups // 2):
            lanes = slice(pair * LANES, (pair + 1) * LANES)
            out = product[pair * LANES : (pair + 1) * LANES, lanes]
            even0, odd0, even1, odd1 = (out[q * HALF : (q + 1) * HALF] for q in range(4))
            mixed = pltpu.roll(jnp.where(low_lanes, odd0, even1), TILE, 1)
            terms[2 * pair, pl.ds(i, HALF, stride=OUT_STRIDE), :] = jnp.where(low_lanes, even0, mixed)
            terms[2 * pair + 1, pl.ds(i, HALF, stride=OUT_STRIDE), :] = jnp.where(low_lanes, mixed, odd1)

    for u in range(groups):
        for m in range(HALF):
            out_ref[u, :, m * LANES : (m + 1) * LANES] = terms[u, m * OUT_STRIDE : m * OUT_STRIDE + ROWS, :].astype(BF16)


def make_terms(y, primal, dual, *slabs):
    order = primal.shape[1]
    tiles = order // TILE
    width = order // SPLIT
    groups = width // TILE
    count = slabs[0].shape[0]
    steps = count // ROWS
    total = count * len(slabs)

    def slab_spec(k):
        return pl.BlockSpec(
            (ROWS, PACKED),
            lambda g, y: (jnp.clip(g - k * steps, 0, steps - 1), 0),
        )

    scratch = [
        pltpu.VMEM((ROWS, 2 * TILE, width), BF16),
        pltpu.VMEM((groups, max(HALF * OUT_STRIDE, ROWS * ROW_STRIDE), LANES), F32),
        pltpu.VMEM((ROWS, LANES), F32),
        pltpu.VMEM((len(slabs), 8, LANES), jnp.int32),
        pltpu.SMEM((len(slabs), 8, LANES), jnp.int32),
        pltpu.VMEM((width, LANES), F32),
        pltpu.VMEM((tiles, 2 * TILE, width), BF16),
        pltpu.VMEM((tiles, width, 4 * TILE), BF16),
    ]
    return pl.pallas_call(
        functools.partial(terms_kernel, len(slabs)),
        out_shape=jax.ShapeDtypeStruct((groups, total, TILE * TILE), BF16),
        grid_spec=pltpu.PrefetchScalarGridSpec(
            num_scalar_prefetch=1,
            grid=(total // ROWS,),
            in_specs=[
                pl.BlockSpec((1, width, order), lambda g, y: (0, y[0], 0)),
                pl.BlockSpec((1, order, width), lambda g, y: (0, 0, y[0])),
                *(slab_spec(k) for k in range(len(slabs))),
                *(
                    pl.BlockSpec((EXTRA, LANES), lambda g, y: (0, TILE * HALF // LANES))
                    for _ in slabs
                ),
            ],
            out_specs=pl.BlockSpec((groups, ROWS, TILE * TILE), lambda g, y: (0, g, 0)),
            scratch_shapes=scratch,
        ),
        compiler_params=pltpu.CompilerParams(vmem_limit_bytes=52 << 20),
        cost_estimate=pl.CostEstimate(
            flops=total * 10**8, transcendentals=0, bytes_accessed=2 * 10**6 + total * 40000
        ),
        name="terms",
    )(y, primal, dual, *slabs, *slabs)


STEP = 1024


def contract_kernel(packed_ref, own_ref, rest_ref, out_ref, turned, weights):
    group = pl.program_id(0)
    count, _, small, _ = packed_ref.shape
    targets, sources, _ = out_ref.shape
    for v in range(PACKED // LANES):
        lanes = slice(v * LANES, (v + 1) * LANES)
        part = packed_ref[:, 0, :, lanes].astype(F32).reshape(count * small, LANES)
        part = part.T
        if v < HALF // 2:
            for k in range(2):
                turned[(2 * v + k) * TURN_STRIDE : (2 * v + k) * TURN_STRIDE + TILE, :] = part[k * TILE : (k + 1) * TILE]
        else:
            turned[HALF * TURN_STRIDE :, :] = part
    place = lax.broadcasted_iota(jnp.int32, (HALF, LANES), 0)
    for e in range(HALF):
        mixed = turned[e * TURN_STRIDE : e * TURN_STRIDE + HALF, :]
        square = turned[e * TURN_STRIDE + HALF : e * TURN_STRIDE + TILE, :]
        mixed_t = turned[pl.ds(e, HALF, stride=TURN_STRIDE), :]
        square_t = turned[pl.ds(HALF + e, HALF, stride=TURN_STRIDE), :]
        start = TURN_STRIDE * HALF + (e % 2) * TILE + e
        diagonal = turned[start : start + 1, :]
        first = jnp.where(place >= e, mixed, mixed_t)
        last = jnp.where(place == e, diagonal, jnp.where(place < e, mixed, mixed_t))
        up = jnp.concatenate([first, square], axis=0)
        low = jnp.concatenate([square_t, last], axis=0)
        weights[e * TILE : (e + 1) * TILE, :] = up.astype(BF16)
        weights[(HALF + e) * TILE : (HALF + e + 1) * TILE, :] = low.astype(BF16)
    left = jnp.concatenate([own_ref[0], rest_ref[0]], axis=0)
    acc = jnp.dot(left, weights[...], preferred_element_type=F32)
    for r in range(targets):
        starts = [(s * targets + r) * 8 for s in range(sources // 8)]
        mine = jnp.concatenate([acc[start : start + 8, :] for start in starts], axis=0)
        out_ref[r] = mine.astype(BF16)


def contract(packed, own, rest, targets):
    count, groups, small, _ = packed.shape
    _, own_rows, width = own.shape
    rest_rows = rest.shape[1]
    total = own_rows + rest_rows
    return pl.pallas_call(
        contract_kernel,
        out_shape=jax.ShapeDtypeStruct((targets, total // targets, groups * LANES), BF16),
        grid_spec=pltpu.PrefetchScalarGridSpec(
            num_scalar_prefetch=0,
            grid=(groups,),
            in_specs=[
                pl.BlockSpec((count, 1, small, PACKED), lambda g: (0, g, 0, 0)),
                pl.BlockSpec((1, own_rows, width), lambda g: (g, 0, 0)),
                pl.BlockSpec((1, rest_rows, width), lambda g: (g, 0, 0)),
            ],
            out_specs=pl.BlockSpec((targets, total // targets, LANES), lambda g: (0, 0, g)),
            scratch_shapes=[
                pltpu.VMEM((TURN_STRIDE * HALF + LANES, LANES), F32),
                pltpu.VMEM((width, LANES), BF16),
            ],
        ),
        compiler_params=pltpu.CompilerParams(vmem_limit_bytes=50 << 20),
        cost_estimate=pl.CostEstimate(flops=6 * 10**9, transcendentals=0, bytes_accessed=2 * 10**7),
        name="contract",
    )(packed, own, rest)


def place_kernel(perm_ref, parts_ref, out_ref, left):
    step = pl.program_id(0)
    sources, rows, width = parts_ref.shape
    total = sources * 8

    @pl.when(step == 0)
    def prepare():
        shared = sources // SPLIT
        for y_s in range(SPLIT):
            arrived = [parts_ref[y_s * shared + z].astype(F32) for z in range(shared)]
            rows = []
            for y in range(SPLIT):
                d = (y_s - y) % SPLIT
                rows += [arrived[z][d * 8 : (d + 1) * 8] for z in range(shared)]
            left[:, y_s * width : (y_s + 1) * width] = jnp.concatenate(rows, axis=0).astype(BF16)

    target = lax.broadcasted_iota(jnp.int32, (STEP, perm_ref.shape[1]), 0) + step * STEP
    chosen = jnp.where(perm_ref[...] == target, 1.0, 0.0).astype(BF16)
    out = lax.dot_general(left[...], chosen, (((1,), (1,)), ((), ())), preferred_element_type=F32)
    for c in range(STEP // LANES):
        out_ref[c] = out[:, c * LANES : (c + 1) * LANES].astype(BF16)


def place(perm, parts):
    sources, rows, width = parts.shape
    columns = perm.shape[1]
    total = sources * 8
    return pl.pallas_call(
        place_kernel,
        out_shape=jax.ShapeDtypeStruct((columns // LANES, total, LANES), BF16),
        grid_spec=pltpu.PrefetchScalarGridSpec(
            num_scalar_prefetch=0,
            grid=(columns // STEP,),
            in_specs=[
                pl.BlockSpec((1, columns), lambda g: (0, 0)),
                pl.BlockSpec((sources, rows, width), lambda g: (0, 0, 0)),
            ],
            out_specs=pl.BlockSpec((STEP // LANES, total, LANES), lambda g: (g, 0, 0)),
            scratch_shapes=[pltpu.VMEM((total, columns), BF16)],
        ),
        compiler_params=pltpu.CompilerParams(vmem_limit_bytes=40 << 20),
        cost_estimate=pl.CostEstimate(flops=2 * 10**9, transcendentals=0, bytes_accessed=10**6),
        name="place",
    )(perm, parts)


def body(row_size, primal, dual_inv, col_values, col_perm, slab_values, slab_tile):
    count = slab_values.shape[1]
    shared = row_size // SPLIT
    block = lax.axis_index("col")
    y = (lax.axis_index("row").astype(jnp.int32) // shared).reshape(1)

    packed = pack(y, col_values)
    packed = lax.all_to_all(packed, "col", split_axis=0, concat_axis=0, tiled=True)

    message = pack_slab(slab_values, slab_tile)
    arrived = []
    for d in range(1, SPLIT):
        pairs = [(i, (i + d * shared) % row_size) for i in range(row_size)]
        arrived.append(lax.ppermute(message, "row", pairs))

    own = make_terms(y, primal, dual_inv, message)
    rest = make_terms(y, primal, dual_inv, *arrived)
    parts = contract(packed, own, rest, row_size)
    parts = lax.all_to_all(parts, "row", split_axis=0, concat_axis=0, tiled=True)
    perm = lax.dynamic_slice_in_dim(col_perm, block, 1, axis=0)
    placed = place(perm, parts)
    placed = lax.all_to_all(placed, "col", split_axis=0, concat_axis=0, tiled=True)
    return jnp.sum(placed.astype(F32), axis=0)


def solution(mesh):
    return jax.shard_map(
        functools.partial(body, mesh.shape["row"]),
        mesh=mesh,
        in_specs=(
            P("col", None, None),
            P("col", None, None),
            P(None, None, "col", None),
            P(),
            P("col", "row", None),
            P("col", "row"),
        ),
        out_specs=P("row", "col"),
        check_vma=False,
    )
```

```python
import functools

import jax
import jax.numpy as jnp
from jax import lax
from jax.experimental import pallas as pl
from jax.experimental.pallas import tpu as pltpu
from jax.sharding import PartitionSpec as P

TILE = 64
HALF = TILE // 2
LANES = 128
PACKED = TILE * HALF + LANES
SPLIT = 4
F32 = jnp.float32
BF16 = jnp.bfloat16


def lane_parts(shape, first_vreg):
    lane = lax.broadcasted_iota(jnp.int32, shape, len(shape) - 1)
    e = lane // TILE + 2 * first_vreg
    h = (lane % TILE) // HALF
    f = lane % HALF
    return e, h, f


def pack_kernel(y_ref, values_ref, slab_ref, tile_ref, out_ref, message_ref):
    @pl.when(pl.program_id(0) == 0)
    def slab_rows():
        pack_slab_kernel(slab_ref, tile_ref, message_ref)

    blocks, groups, rows, width = values_ref.shape
    half = width // 2
    count = blocks * groups * rows
    for j in range(half // LANES):
        lanes = slice(j * LANES, (j + 1) * LANES)
        e, h, f = lane_parts((count, LANES), j)
        upper = values_ref[:, :, :, lanes].astype(F32).reshape(count, LANES)
        lower = values_ref[:, :, :, half + j * LANES : half + (j + 1) * LANES].astype(F32).reshape(count, LANES)
        lower = pltpu.roll(lower, LANES - HALF, 1)
        kept = jnp.where((h == 1) | (e <= f), upper, lower)
        extra = jnp.where((h == 0) & (e == f), lower, 0.0 if j == 0 else extra)
        out_ref[:, :, :, lanes] = kept.reshape(blocks, groups, rows, LANES).astype(BF16)
    out_ref[:, :, :, half:] = extra.reshape(blocks, groups, rows, LANES).astype(BF16)


def pack(y, values, slab, tile_of):
    _, count, slab_width = slab.shape
    blocks, tiles, rows, width = values.shape
    groups = tiles // SPLIT
    step = blocks // 2
    return pl.pallas_call(
        pack_kernel,
        out_shape=[
            jax.ShapeDtypeStruct((blocks, groups, rows, PACKED), BF16),
            jax.ShapeDtypeStruct((count, PACKED), BF16),
        ],
        grid_spec=pltpu.PrefetchScalarGridSpec(
            num_scalar_prefetch=1,
            grid=(blocks // step,),
            in_specs=[
                pl.BlockSpec((step, groups, rows, width), lambda g, y: (g, y[0], 0, 0)),
                pl.BlockSpec((1, count, slab_width), lambda g, y: (0, 0, 0)),
                pl.BlockSpec((1, count), lambda g, y: (0, 0)),
            ],
            out_specs=[
                pl.BlockSpec((step, groups, rows, PACKED), lambda g, y: (g, 0, 0, 0)),
                pl.BlockSpec((count, PACKED), lambda g, y: (0, 0)),
            ],
        ),
        compiler_params=pltpu.CompilerParams(vmem_limit_bytes=59 << 20),
        cost_estimate=pl.CostEstimate(flops=10**7, transcendentals=0, bytes_accessed=7 * 10**6),
        name="pack",
    )(y, values, slab, tile_of)


def pack_slab_kernel(slab_ref, tile_ref, out_ref):
    half = slab_ref.shape[2] // 2
    count = slab_ref.shape[1]
    extra = jnp.zeros((count, LANES), F32)
    for j in range(half // LANES):
        e, h, f = lane_parts((count, LANES), j)
        upper = slab_ref[0, :, j * LANES : (j + 1) * LANES].astype(F32)
        lower = slab_ref[0, :, half + j * LANES : half + (j + 1) * LANES].astype(F32)
        lower = pltpu.roll(lower, LANES - HALF, 1)
        kept = jnp.where((h == 1) | (e <= f), upper, lower)
        extra = jnp.where((h == 0) & (e == f), lower, extra)
        out_ref[:, j * LANES : (j + 1) * LANES] = kept.astype(BF16)
    ids = tile_ref[...].astype(F32)
    ids = jnp.concatenate([jnp.zeros((1, LANES - count), F32), ids], axis=1)
    lane = lax.broadcasted_iota(jnp.int32, (count, LANES), 1)
    extra = extra + jnp.where(lane < TILE, pltpu.roll(extra, TILE, 1), 0.0)
    out_ref[:, half:] = jnp.where(lane < TILE, extra, ids).astype(BF16)


def split2(x):
    high = x.astype(BF16)
    low = (x - high.astype(F32)).astype(BF16)
    return high, low


ROWS = 64
EXTRA = 16
OUT_STRIDE = 72
ROW_STRIDE = 40
TURN_STRIDE = 72


def terms_kernel(parts, y_ref, primal_ref, dual_ref, *refs):
    slabs, tile_rows, refs = refs[:parts], refs[parts : 2 * parts], refs[2 * parts :]
    out_ref, weights, terms, diagonals, tile_rows_i, tile_ids, stage, dual_w, primal_w = refs
    tiles = dual_w.shape[0]
    groups = out_ref.shape[0]
    step = pl.program_id(0)
    steps = pl.num_programs(0) // len(slabs)
    lane_i = lax.broadcasted_iota(jnp.int32, (HALF, LANES), 1)
    row_i = lax.broadcasted_iota(jnp.int32, (HALF, LANES), 0)
    lane_i2 = lax.broadcasted_iota(jnp.int32, (TILE, LANES), 1)
    low_lanes = lane_i < TILE

    @pl.when(step == 0)
    def prepare():
        for k in range(parts):
            tile_rows_i[k] = tile_rows[k][...].astype(F32).astype(jnp.int32)[:8]
        pltpu.sync_copy(tile_rows_i, tile_ids)
        for t in range(tiles):
            high, low = split2(dual_ref[0, t * TILE : (t + 1) * TILE, :])
            dual_w[t, :TILE, :] = high
            dual_w[t, TILE:, :] = low
        source = lax.broadcasted_iota(jnp.int32, (LANES, 2 * LANES), 0)
        target = lax.broadcasted_iota(jnp.int32, (LANES, 2 * LANES), 1)
        wanted = (target // LANES) * TILE + target % TILE
        spread = jnp.where(source == wanted, 1.0, 0.0).astype(BF16)
        for j in range(tiles // 2):
            stage[...] = primal_ref[0, :, j * LANES : (j + 1) * LANES]
            x = jnp.concatenate(
                [
                    stage[pl.ds(u * TILE + par, HALF, stride=2), :]
                    for u in range(groups)
                    for par in range(2)
                ],
                axis=0,
            )
            for place, part in enumerate(split2(x)):
                part = jnp.dot(part, spread, preferred_element_type=F32).astype(BF16)
                lanes = slice(place * LANES, (place + 1) * LANES)
                primal_w[2 * j, :, lanes] = part[:, :LANES]
                primal_w[2 * j + 1, :, lanes] = part[:, LANES:]

    for k, slab_ref in enumerate(slabs):

        @pl.when(step // steps == k)
        def spread_rows():
            for m in range(HALF // 2):
                part = slab_ref[:, m * LANES : (m + 1) * LANES].astype(F32)
                terms[0, pl.ds(2 * m, ROWS, stride=ROW_STRIDE), :] = part
                terms[0, pl.ds(2 * m + 1, ROWS, stride=ROW_STRIDE), :] = pltpu.roll(part, TILE, 1)
            diagonals[...] = slab_ref[:, TILE * HALF :].astype(F32)

    tile_of = [tile_ids[step // steps, 0, TILE + (step % steps) * ROWS + i] for i in range(ROWS)]

    for i in range(ROWS):
        z = terms[0, i * ROW_STRIDE : i * ROW_STRIDE + HALF, :]
        turned = z.T
        z_t = jnp.concatenate([turned[:HALF], jnp.zeros((HALF, LANES - HALF), F32)], axis=1)
        square_t = jnp.concatenate([turned[HALF:TILE], jnp.zeros((HALF, LANES - HALF), F32)], axis=1)
        top = jnp.where(lane_i >= row_i, z, z_t)
        corner = jnp.where(lane_i < row_i, z, z_t)
        corner = jnp.where(lane_i == row_i, diagonals[i : i + 1, :], corner)
        bottom = jnp.where(lane_i < HALF, square_t, pltpu.roll(corner, HALF, 1))
        square = jnp.concatenate([top, bottom], axis=0)
        square = jnp.where(lane_i2 < TILE, square, pltpu.roll(square, TILE, 1)).astype(BF16)
        panel = jnp.dot(square, dual_w[tile_of[i]], preferred_element_type=F32)
        high, low = split2(panel)
        weights[i, :TILE, :] = high
        weights[i, TILE:, :] = low

    for i in range(ROWS):
        t = tile_of[i]
        right = weights[i]
        product = jnp.dot(primal_w[t], jnp.concatenate([right, right], axis=0), preferred_element_type=F32)
        for pair in range(groups // 2):
            lanes = slice(pair * LANES, (pair + 1) * LANES)
            out = product[pair * LANES : (pair + 1) * LANES, lanes]
            even0, odd0, even1, odd1 = (out[q * HALF : (q + 1) * HALF] for q in range(4))
            mixed = pltpu.roll(jnp.where(low_lanes, odd0, even1), TILE, 1)
            terms[2 * pair, pl.ds(i, HALF, stride=OUT_STRIDE), :] = jnp.where(low_lanes, even0, mixed)
            terms[2 * pair + 1, pl.ds(i, HALF, stride=OUT_STRIDE), :] = jnp.where(low_lanes, mixed, odd1)

    for u in range(groups):
        for m in range(HALF):
            out_ref[u, :, m * LANES : (m + 1) * LANES] = terms[u, m * OUT_STRIDE : m * OUT_STRIDE + ROWS, :].astype(BF16)


def make_terms(y, primal, dual, *slabs):
    order = primal.shape[1]
    tiles = order // TILE
    width = order // SPLIT
    groups = width // TILE
    count = slabs[0].shape[0]
    steps = count // ROWS
    total = count * len(slabs)

    def slab_spec(k):
        return pl.BlockSpec(
            (ROWS, PACKED),
            lambda g, y: (jnp.clip(g - k * steps, 0, steps - 1), 0),
        )

    scratch = [
        pltpu.VMEM((ROWS, 2 * TILE, width), BF16),
        pltpu.VMEM((groups, max(HALF * OUT_STRIDE, ROWS * ROW_STRIDE), LANES), F32),
        pltpu.VMEM((ROWS, LANES), F32),
        pltpu.VMEM((len(slabs), 8, LANES), jnp.int32),
        pltpu.SMEM((len(slabs), 8, LANES), jnp.int32),
        pltpu.VMEM((width, LANES), F32),
        pltpu.VMEM((tiles, 2 * TILE, width), BF16),
        pltpu.VMEM((tiles, width, 4 * TILE), BF16),
    ]
    return pl.pallas_call(
        functools.partial(terms_kernel, len(slabs)),
        out_shape=jax.ShapeDtypeStruct((groups, total, TILE * TILE), BF16),
        grid_spec=pltpu.PrefetchScalarGridSpec(
            num_scalar_prefetch=1,
            grid=(total // ROWS,),
            in_specs=[
                pl.BlockSpec((1, width, order), lambda g, y: (0, y[0], 0)),
                pl.BlockSpec((1, order, width), lambda g, y: (0, 0, y[0])),
                *(slab_spec(k) for k in range(len(slabs))),
                *(
                    pl.BlockSpec((EXTRA, LANES), lambda g, y: (0, TILE * HALF // LANES))
                    for _ in slabs
                ),
            ],
            out_specs=pl.BlockSpec((groups, ROWS, TILE * TILE), lambda g, y: (0, g, 0)),
            scratch_shapes=scratch,
        ),
        compiler_params=pltpu.CompilerParams(vmem_limit_bytes=52 << 20),
        cost_estimate=pl.CostEstimate(
            flops=total * 10**8, transcendentals=0, bytes_accessed=2 * 10**6 + total * 40000
        ),
        name="terms",
    )(y, primal, dual, *slabs, *slabs)


STEP = 1024


def contract_kernel(packed_ref, own_ref, rest_ref, out_ref, turned, weights):
    group = pl.program_id(0)
    count, _, small, _ = packed_ref.shape
    targets, sources, _ = out_ref.shape
    for v in range(PACKED // LANES):
        lanes = slice(v * LANES, (v + 1) * LANES)
        part = packed_ref[:, 0, :, lanes].astype(F32).reshape(count * small, LANES)
        part = part.T
        if v < HALF // 2:
            for k in range(2):
                turned[(2 * v + k) * TURN_STRIDE : (2 * v + k) * TURN_STRIDE + TILE, :] = part[k * TILE : (k + 1) * TILE]
        else:
            turned[HALF * TURN_STRIDE :, :] = part
    place = lax.broadcasted_iota(jnp.int32, (HALF, LANES), 0)
    for e in range(HALF):
        mixed = turned[e * TURN_STRIDE : e * TURN_STRIDE + HALF, :]
        square = turned[e * TURN_STRIDE + HALF : e * TURN_STRIDE + TILE, :]
        mixed_t = turned[pl.ds(e, HALF, stride=TURN_STRIDE), :]
        square_t = turned[pl.ds(HALF + e, HALF, stride=TURN_STRIDE), :]
        start = TURN_STRIDE * HALF + (e % 2) * TILE + e
        diagonal = turned[start : start + 1, :]
        first = jnp.where(place >= e, mixed, mixed_t)
        last = jnp.where(place == e, diagonal, jnp.where(place < e, mixed, mixed_t))
        up = jnp.concatenate([first, square], axis=0)
        low = jnp.concatenate([square_t, last], axis=0)
        weights[e * TILE : (e + 1) * TILE, :] = up.astype(BF16)
        weights[(HALF + e) * TILE : (HALF + e + 1) * TILE, :] = low.astype(BF16)
    left = jnp.concatenate([own_ref[0], rest_ref[0]], axis=0)
    acc = jnp.dot(left, weights[...], preferred_element_type=F32)
    for r in range(targets):
        starts = [(s * targets + r) * 8 for s in range(sources // 8)]
        mine = jnp.concatenate([acc[start : start + 8, :] for start in starts], axis=0)
        out_ref[r] = mine.astype(BF16)


def contract(packed, own, rest, targets):
    count, groups, small, _ = packed.shape
    _, own_rows, width = own.shape
    rest_rows = rest.shape[1]
    total = own_rows + rest_rows
    return pl.pallas_call(
        contract_kernel,
        out_shape=jax.ShapeDtypeStruct((targets, total // targets, groups * LANES), BF16),
        grid_spec=pltpu.PrefetchScalarGridSpec(
            num_scalar_prefetch=0,
            grid=(groups,),
            in_specs=[
                pl.BlockSpec((count, 1, small, PACKED), lambda g: (0, g, 0, 0)),
                pl.BlockSpec((1, own_rows, width), lambda g: (g, 0, 0)),
                pl.BlockSpec((1, rest_rows, width), lambda g: (g, 0, 0)),
            ],
            out_specs=pl.BlockSpec((targets, total // targets, LANES), lambda g: (0, 0, g)),
            scratch_shapes=[
                pltpu.VMEM((TURN_STRIDE * HALF + LANES, LANES), F32),
                pltpu.VMEM((width, LANES), BF16),
            ],
        ),
        compiler_params=pltpu.CompilerParams(vmem_limit_bytes=50 << 20),
        cost_estimate=pl.CostEstimate(flops=6 * 10**9, transcendentals=0, bytes_accessed=2 * 10**7),
        name="contract",
    )(packed, own, rest)


def place_kernel(perm_ref, parts_ref, out_ref, left):
    step = pl.program_id(0)
    sources, rows, width = parts_ref.shape
    total = sources * 8

    @pl.when(step == 0)
    def prepare():
        shared = sources // SPLIT
        for y_s in range(SPLIT):
            arrived = [parts_ref[y_s * shared + z].astype(F32) for z in range(shared)]
            rows = []
            for y in range(SPLIT):
                d = (y_s - y) % SPLIT
                rows += [arrived[z][d * 8 : (d + 1) * 8] for z in range(shared)]
            left[:, y_s * width : (y_s + 1) * width] = jnp.concatenate(rows, axis=0).astype(BF16)

    target = lax.broadcasted_iota(jnp.int32, (STEP, perm_ref.shape[1]), 0) + step * STEP
    chosen = jnp.where(perm_ref[...] == target, 1.0, 0.0).astype(BF16)
    out = lax.dot_general(left[...], chosen, (((1,), (1,)), ((), ())), preferred_element_type=F32)
    for c in range(STEP // LANES):
        out_ref[c] = out[:, c * LANES : (c + 1) * LANES].astype(BF16)


def place(perm, parts):
    sources, rows, width = parts.shape
    columns = perm.shape[1]
    total = sources * 8
    return pl.pallas_call(
        place_kernel,
        out_shape=jax.ShapeDtypeStruct((columns // LANES, total, LANES), BF16),
        grid_spec=pltpu.PrefetchScalarGridSpec(
            num_scalar_prefetch=0,
            grid=(columns // STEP,),
            in_specs=[
                pl.BlockSpec((1, columns), lambda g: (0, 0)),
                pl.BlockSpec((sources, rows, width), lambda g: (0, 0, 0)),
            ],
            out_specs=pl.BlockSpec((STEP // LANES, total, LANES), lambda g: (g, 0, 0)),
            scratch_shapes=[pltpu.VMEM((total, columns), BF16)],
        ),
        compiler_params=pltpu.CompilerParams(vmem_limit_bytes=40 << 20),
        cost_estimate=pl.CostEstimate(flops=2 * 10**9, transcendentals=0, bytes_accessed=10**6),
        name="place",
    )(perm, parts)


def body(row_size, primal, dual_inv, col_values, col_perm, slab_values, slab_tile):
    count = slab_values.shape[1]
    shared = row_size // SPLIT
    block = lax.axis_index("col")
    y = (lax.axis_index("row").astype(jnp.int32) // shared).reshape(1)

    packed, message = pack(y, col_values, slab_values, slab_tile)
    packed = lax.all_to_all(packed, "col", split_axis=0, concat_axis=0, tiled=True)

    arrived = []
    for d in range(1, SPLIT):
        pairs = [(i, (i + d * shared) % row_size) for i in range(row_size)]
        arrived.append(lax.ppermute(message, "row", pairs))

    own = make_terms(y, primal, dual_inv, message)
    rest = make_terms(y, primal, dual_inv, *arrived)
    parts = contract(packed, own, rest, row_size)
    parts = lax.all_to_all(parts, "row", split_axis=0, concat_axis=0, tiled=True)
    perm = lax.dynamic_slice_in_dim(col_perm, block, 1, axis=0)
    placed = place(perm, parts)
    placed = lax.all_to_all(placed, "col", split_axis=0, concat_axis=0, tiled=True)
    return jnp.sum(placed.astype(F32), axis=0)


def solution(mesh):
    return jax.shard_map(
        functools.partial(body, mesh.shape["row"]),
        mesh=mesh,
        in_specs=(
            P("col", None, None),
            P("col", None, None),
            P(None, None, "col", None),
            P(),
            P("col", "row", None),
            P("col", "row"),
        ),
        out_specs=P("row", "col"),
        check_vma=False,
    )
```

```python
import functools

import jax
import jax.numpy as jnp
from jax import lax
from jax.experimental import pallas as pl
from jax.experimental.pallas import tpu as pltpu
from jax.sharding import PartitionSpec as P

TILE = 64
HALF = TILE // 2
LANES = 128
PACKED = TILE * HALF + LANES
SPLIT = 4
F32 = jnp.float32
BF16 = jnp.bfloat16


def lane_parts(shape, first_vreg):
    lane = lax.broadcasted_iota(jnp.int32, shape, len(shape) - 1)
    e = lane // TILE + 2 * first_vreg
    h = (lane % TILE) // HALF
    f = lane % HALF
    return e, h, f


def pack_kernel(y_ref, values_ref, slab_ref, tile_ref, out_ref, message_ref):
    @pl.when(pl.program_id(0) == 0)
    def slab_rows():
        pack_slab_kernel(slab_ref, tile_ref, message_ref)

    blocks, groups, rows, width = values_ref.shape
    half = width // 2
    count = blocks * groups * rows
    for j in range(half // LANES):
        lanes = slice(j * LANES, (j + 1) * LANES)
        e, h, f = lane_parts((count, LANES), j)
        upper = values_ref[:, :, :, lanes].astype(F32).reshape(count, LANES)
        lower = values_ref[:, :, :, half + j * LANES : half + (j + 1) * LANES].astype(F32).reshape(count, LANES)
        lower = pltpu.roll(lower, LANES - HALF, 1)
        kept = jnp.where((h == 1) | (e <= f), upper, lower)
        extra = jnp.where((h == 0) & (e == f), lower, 0.0 if j == 0 else extra)
        out_ref[:, :, :, lanes] = kept.reshape(blocks, groups, rows, LANES).astype(BF16)
    out_ref[:, :, :, half:] = extra.reshape(blocks, groups, rows, LANES).astype(BF16)


def pack(y, values, slab, tile_of):
    _, count, slab_width = slab.shape
    blocks, tiles, rows, width = values.shape
    groups = tiles // SPLIT
    step = blocks // 2
    return pl.pallas_call(
        pack_kernel,
        out_shape=[
            jax.ShapeDtypeStruct((blocks, groups, rows, PACKED), BF16),
            jax.ShapeDtypeStruct((count, PACKED), BF16),
        ],
        grid_spec=pltpu.PrefetchScalarGridSpec(
            num_scalar_prefetch=1,
            grid=(blocks // step,),
            in_specs=[
                pl.BlockSpec((step, groups, rows, width), lambda g, y: (g, y[0], 0, 0)),
                pl.BlockSpec((1, count, slab_width), lambda g, y: (0, 0, 0)),
                pl.BlockSpec((1, count), lambda g, y: (0, 0)),
            ],
            out_specs=[
                pl.BlockSpec((step, groups, rows, PACKED), lambda g, y: (g, 0, 0, 0)),
                pl.BlockSpec((count, PACKED), lambda g, y: (0, 0)),
            ],
        ),
        compiler_params=pltpu.CompilerParams(vmem_limit_bytes=59 << 20),
        cost_estimate=pl.CostEstimate(flops=10**7, transcendentals=0, bytes_accessed=7 * 10**6),
        name="pack",
    )(y, values, slab, tile_of)


def pack_slab_kernel(slab_ref, tile_ref, out_ref):
    half = slab_ref.shape[2] // 2
    count = slab_ref.shape[1]
    extra = jnp.zeros((count, LANES), F32)
    for j in range(half // LANES):
        e, h, f = lane_parts((count, LANES), j)
        upper = slab_ref[0, :, j * LANES : (j + 1) * LANES].astype(F32)
        lower = slab_ref[0, :, half + j * LANES : half + (j + 1) * LANES].astype(F32)
        lower = pltpu.roll(lower, LANES - HALF, 1)
        kept = jnp.where((h == 1) | (e <= f), upper, lower)
        extra = jnp.where((h == 0) & (e == f), lower, extra)
        out_ref[:, j * LANES : (j + 1) * LANES] = kept.astype(BF16)
    ids = tile_ref[...].astype(F32)
    ids = jnp.concatenate([jnp.zeros((1, LANES - count), F32), ids], axis=1)
    lane = lax.broadcasted_iota(jnp.int32, (count, LANES), 1)
    extra = extra + jnp.where(lane < TILE, pltpu.roll(extra, TILE, 1), 0.0)
    out_ref[:, half:] = jnp.where(lane < TILE, extra, ids).astype(BF16)


def split2(x):
    high = x.astype(BF16)
    low = (x - high.astype(F32)).astype(BF16)
    return high, low


ROWS = 64
EXTRA = 16
OUT_STRIDE = 72
ROW_STRIDE = 40
TURN_STRIDE = 72


def terms_kernel(parts, y_ref, primal_ref, dual_ref, *refs):
    slabs, tile_rows, refs = refs[:parts], refs[parts : 2 * parts], refs[2 * parts :]
    out_ref, weights, terms, diagonals, tile_rows_i, tile_ids, stage, dual_w, primal_w = refs
    tiles = dual_w.shape[0]
    groups = out_ref.shape[0]
    step = pl.program_id(0)
    steps = pl.num_programs(0) // len(slabs)
    lane_i = lax.broadcasted_iota(jnp.int32, (HALF, LANES), 1)
    row_i = lax.broadcasted_iota(jnp.int32, (HALF, LANES), 0)
    lane_i2 = lax.broadcasted_iota(jnp.int32, (TILE, LANES), 1)
    low_lanes = lane_i < TILE

    @pl.when(step == 0)
    def prepare():
        for k in range(parts):
            tile_rows_i[k] = tile_rows[k][...].astype(F32).astype(jnp.int32)[:8]
        pltpu.sync_copy(tile_rows_i, tile_ids)
        for t in range(tiles):
            high, low = split2(dual_ref[0, t * TILE : (t + 1) * TILE, :])
            dual_w[t, :TILE, :] = high
            dual_w[t, TILE:, :] = low
        source = lax.broadcasted_iota(jnp.int32, (LANES, 2 * LANES), 0)
        target = lax.broadcasted_iota(jnp.int32, (LANES, 2 * LANES), 1)
        wanted = (target // LANES) * TILE + target % TILE
        spread = jnp.where(source == wanted, 1.0, 0.0).astype(BF16)
        for j in range(tiles // 2):
            stage[...] = primal_ref[0, :, j * LANES : (j + 1) * LANES]
            x = jnp.concatenate(
                [
                    stage[pl.ds(u * TILE + par, HALF, stride=2), :]
                    for u in range(groups)
                    for par in range(2)
                ],
                axis=0,
            )
            for place, part in enumerate(split2(x)):
                part = jnp.dot(part, spread, preferred_element_type=F32).astype(BF16)
                lanes = slice(place * LANES, (place + 1) * LANES)
                primal_w[2 * j, :, lanes] = part[:, :LANES]
                primal_w[2 * j + 1, :, lanes] = part[:, LANES:]

    for k, slab_ref in enumerate(slabs):

        @pl.when(step // steps == k)
        def spread_rows():
            for m in range(HALF // 2):
                part = slab_ref[:, m * LANES : (m + 1) * LANES].astype(F32)
                terms[0, pl.ds(2 * m, ROWS, stride=ROW_STRIDE), :] = part
                terms[0, pl.ds(2 * m + 1, ROWS, stride=ROW_STRIDE), :] = pltpu.roll(part, TILE, 1)
            diagonals[...] = slab_ref[:, TILE * HALF :].astype(F32)

    tile_of = [tile_ids[step // steps, 0, TILE + (step % steps) * ROWS + i] for i in range(ROWS)]

    for i in range(ROWS):
        z = terms[0, i * ROW_STRIDE : i * ROW_STRIDE + HALF, :]
        turned = z.T
        z_t = jnp.concatenate([turned[:HALF], jnp.zeros((HALF, LANES - HALF), F32)], axis=1)
        square_t = jnp.concatenate([turned[HALF:TILE], jnp.zeros((HALF, LANES - HALF), F32)], axis=1)
        top = jnp.where(lane_i >= row_i, z, z_t)
        corner = jnp.where(lane_i < row_i, z, z_t)
        corner = jnp.where(lane_i == row_i, diagonals[i : i + 1, :], corner)
        bottom = jnp.where(lane_i < HALF, square_t, pltpu.roll(corner, HALF, 1))
        square = jnp.concatenate([top, bottom], axis=0)
        square = jnp.where(lane_i2 < TILE, square, pltpu.roll(square, TILE, 1)).astype(BF16)
        panel = jnp.dot(square, dual_w[tile_of[i]], preferred_element_type=F32)
        high, low = split2(panel)
        weights[i, :TILE, :] = high
        weights[i, TILE:, :] = low

    for i in range(ROWS):
        t = tile_of[i]
        right = weights[i]
        product = jnp.dot(primal_w[t], jnp.concatenate([right, right], axis=0), preferred_element_type=F32)
        for pair in range(groups // 2):
            lanes = slice(pair * LANES, (pair + 1) * LANES)
            out = product[pair * LANES : (pair + 1) * LANES, lanes]
            even0, odd0, even1, odd1 = (out[q * HALF : (q + 1) * HALF] for q in range(4))
            mixed = pltpu.roll(jnp.where(low_lanes, odd0, even1), TILE, 1)
            terms[2 * pair, pl.ds(i, HALF, stride=OUT_STRIDE), :] = jnp.where(low_lanes, even0, mixed)
            terms[2 * pair + 1, pl.ds(i, HALF, stride=OUT_STRIDE), :] = jnp.where(low_lanes, mixed, odd1)

    for u in range(groups):
        for m in range(HALF):
            out_ref[u, :, m * LANES : (m + 1) * LANES] = terms[u, m * OUT_STRIDE : m * OUT_STRIDE + ROWS, :].astype(BF16)


def make_terms(y, primal, dual, *slabs):
    order = primal.shape[1]
    tiles = order // TILE
    width = order // SPLIT
    groups = width // TILE
    count = slabs[0].shape[0]
    steps = count // ROWS
    total = count * len(slabs)

    def slab_spec(k):
        return pl.BlockSpec(
            (ROWS, PACKED),
            lambda g, y: (jnp.clip(g - k * steps, 0, steps - 1), 0),
        )

    scratch = [
        pltpu.VMEM((ROWS, 2 * TILE, width), BF16),
        pltpu.VMEM((groups, max(HALF * OUT_STRIDE, ROWS * ROW_STRIDE), LANES), F32),
        pltpu.VMEM((ROWS, LANES), F32),
        pltpu.VMEM((len(slabs), 8, LANES), jnp.int32),
        pltpu.SMEM((len(slabs), 8, LANES), jnp.int32),
        pltpu.VMEM((width, LANES), F32),
        pltpu.VMEM((tiles, 2 * TILE, width), BF16),
        pltpu.VMEM((tiles, width, 4 * TILE), BF16),
    ]
    return pl.pallas_call(
        functools.partial(terms_kernel, len(slabs)),
        out_shape=jax.ShapeDtypeStruct((groups, total, TILE * TILE), BF16),
        grid_spec=pltpu.PrefetchScalarGridSpec(
            num_scalar_prefetch=1,
            grid=(total // ROWS,),
            in_specs=[
                pl.BlockSpec((1, width, order), lambda g, y: (0, y[0], 0)),
                pl.BlockSpec((1, order, width), lambda g, y: (0, 0, y[0])),
                *(slab_spec(k) for k in range(len(slabs))),
                *(
                    pl.BlockSpec((EXTRA, LANES), lambda g, y: (0, TILE * HALF // LANES))
                    for _ in slabs
                ),
            ],
            out_specs=pl.BlockSpec((groups, ROWS, TILE * TILE), lambda g, y: (0, g, 0)),
            scratch_shapes=scratch,
        ),
        compiler_params=pltpu.CompilerParams(vmem_limit_bytes=52 << 20),
        cost_estimate=pl.CostEstimate(
            flops=total * 10**8, transcendentals=0, bytes_accessed=2 * 10**6 + total * 40000
        ),
        name="terms",
    )(y, primal, dual, *slabs, *slabs)


STEP = 2048


def contract_kernel(packed_ref, own_ref, rest_ref, out_ref, turned, weights):
    group = pl.program_id(0)
    count, _, small, _ = packed_ref.shape
    targets, sources, _ = out_ref.shape
    for v in range(PACKED // LANES):
        lanes = slice(v * LANES, (v + 1) * LANES)
        part = packed_ref[:, 0, :, lanes].astype(F32).reshape(count * small, LANES)
        part = part.T
        if v < HALF // 2:
            for k in range(2):
                turned[(2 * v + k) * TURN_STRIDE : (2 * v + k) * TURN_STRIDE + TILE, :] = part[k * TILE : (k + 1) * TILE]
        else:
            turned[HALF * TURN_STRIDE :, :] = part
    place = lax.broadcasted_iota(jnp.int32, (HALF, LANES), 0)
    for e in range(HALF):
        mixed = turned[e * TURN_STRIDE : e * TURN_STRIDE + HALF, :]
        square = turned[e * TURN_STRIDE + HALF : e * TURN_STRIDE + TILE, :]
        mixed_t = turned[pl.ds(e, HALF, stride=TURN_STRIDE), :]
        square_t = turned[pl.ds(HALF + e, HALF, stride=TURN_STRIDE), :]
        start = TURN_STRIDE * HALF + (e % 2) * TILE + e
        diagonal = turned[start : start + 1, :]
        first = jnp.where(place >= e, mixed, mixed_t)
        last = jnp.where(place == e, diagonal, jnp.where(place < e, mixed, mixed_t))
        up = jnp.concatenate([first, square], axis=0)
        low = jnp.concatenate([square_t, last], axis=0)
        weights[e * TILE : (e + 1) * TILE, :] = up.astype(BF16)
        weights[(HALF + e) * TILE : (HALF + e + 1) * TILE, :] = low.astype(BF16)
    left = jnp.concatenate([own_ref[0], rest_ref[0]], axis=0)
    acc = jnp.dot(left, weights[...], preferred_element_type=F32)
    for r in range(targets):
        starts = [(s * targets + r) * 8 for s in range(sources // 8)]
        mine = jnp.concatenate([acc[start : start + 8, :] for start in starts], axis=0)
        out_ref[r] = mine.astype(BF16)


def contract(packed, own, rest, targets):
    count, groups, small, _ = packed.shape
    _, own_rows, width = own.shape
    rest_rows = rest.shape[1]
    total = own_rows + rest_rows
    return pl.pallas_call(
        contract_kernel,
        out_shape=jax.ShapeDtypeStruct((targets, total // targets, groups * LANES), BF16),
        grid_spec=pltpu.PrefetchScalarGridSpec(
            num_scalar_prefetch=0,
            grid=(groups,),
            in_specs=[
                pl.BlockSpec((count, 1, small, PACKED), lambda g: (0, g, 0, 0)),
                pl.BlockSpec((1, own_rows, width), lambda g: (g, 0, 0)),
                pl.BlockSpec((1, rest_rows, width), lambda g: (g, 0, 0)),
            ],
            out_specs=pl.BlockSpec((targets, total // targets, LANES), lambda g: (0, 0, g)),
            scratch_shapes=[
                pltpu.VMEM((TURN_STRIDE * HALF + LANES, LANES), F32),
                pltpu.VMEM((width, LANES), BF16),
            ],
        ),
        compiler_params=pltpu.CompilerParams(vmem_limit_bytes=50 << 20),
        cost_estimate=pl.CostEstimate(flops=6 * 10**9, transcendentals=0, bytes_accessed=2 * 10**7),
        name="contract",
    )(packed, own, rest)


def place_kernel(perm_ref, parts_ref, out_ref, left):
    step = pl.program_id(0)
    sources, rows, width = parts_ref.shape
    total = sources * 8

    @pl.when(step == 0)
    def prepare():
        shared = sources // SPLIT
        for y_s in range(SPLIT):
            arrived = [parts_ref[y_s * shared + z].astype(F32) for z in range(shared)]
            rows = []
            for y in range(SPLIT):
                d = (y_s - y) % SPLIT
                rows += [arrived[z][d * 8 : (d + 1) * 8] for z in range(shared)]
            left[:, y_s * width : (y_s + 1) * width] = jnp.concatenate(rows, axis=0).astype(BF16)

    target = lax.broadcasted_iota(jnp.int32, (STEP, perm_ref.shape[1]), 0) + step * STEP
    chosen = jnp.where(perm_ref[...] == target, 1.0, 0.0).astype(BF16)
    out = lax.dot_general(left[...], chosen, (((1,), (1,)), ((), ())), preferred_element_type=F32)
    for c in range(STEP // LANES):
        out_ref[c] = out[:, c * LANES : (c + 1) * LANES].astype(BF16)


def place(perm, parts):
    sources, rows, width = parts.shape
    columns = perm.shape[1]
    total = sources * 8
    return pl.pallas_call(
        place_kernel,
        out_shape=jax.ShapeDtypeStruct((columns // LANES, total, LANES), BF16),
        grid_spec=pltpu.PrefetchScalarGridSpec(
            num_scalar_prefetch=0,
            grid=(columns // STEP,),
            in_specs=[
                pl.BlockSpec((1, columns), lambda g: (0, 0)),
                pl.BlockSpec((sources, rows, width), lambda g: (0, 0, 0)),
            ],
            out_specs=pl.BlockSpec((STEP // LANES, total, LANES), lambda g: (g, 0, 0)),
            scratch_shapes=[pltpu.VMEM((total, columns), BF16)],
        ),
        compiler_params=pltpu.CompilerParams(vmem_limit_bytes=40 << 20),
        cost_estimate=pl.CostEstimate(flops=2 * 10**9, transcendentals=0, bytes_accessed=10**6),
        name="place",
    )(perm, parts)


def body(row_size, primal, dual_inv, col_values, col_perm, slab_values, slab_tile):
    count = slab_values.shape[1]
    shared = row_size // SPLIT
    block = lax.axis_index("col")
    y = (lax.axis_index("row").astype(jnp.int32) // shared).reshape(1)

    packed, message = pack(y, col_values, slab_values, slab_tile)
    packed = lax.all_to_all(packed, "col", split_axis=0, concat_axis=0, tiled=True)

    arrived = []
    for d in range(1, SPLIT):
        pairs = [(i, (i + d * shared) % row_size) for i in range(row_size)]
        arrived.append(lax.ppermute(message, "row", pairs))

    own = make_terms(y, primal, dual_inv, message)
    rest = make_terms(y, primal, dual_inv, *arrived)
    parts = contract(packed, own, rest, row_size)
    parts = lax.all_to_all(parts, "row", split_axis=0, concat_axis=0, tiled=True)
    perm = lax.dynamic_slice_in_dim(col_perm, block, 1, axis=0)
    placed = place(perm, parts)
    placed = lax.all_to_all(placed, "col", split_axis=0, concat_axis=0, tiled=True)
    return jnp.sum(placed.astype(F32), axis=0)


def solution(mesh):
    return jax.shard_map(
        functools.partial(body, mesh.shape["row"]),
        mesh=mesh,
        in_specs=(
            P("col", None, None),
            P("col", None, None),
            P(None, None, "col", None),
            P(),
            P("col", "row", None),
            P("col", "row"),
        ),
        out_specs=P("row", "col"),
        check_vma=False,
    )
```
